128 devices in a mesh: dom: 16 (over x, y), tool: 8 (over z, core).
Axes of the slice: x: 4, y: 4, z: 4, core: 2. Of those that a mesh axis runs over, the one named last changes fastest.
Arguments:
- records: float32 [8192, 512], P(('dom', 'tool')), may hold values from -6 to 6
- tool_data: float32 [32768, 512], P(('dom', 'tool')), may hold values from -6 to 6
- owners: int32 [8192, 2], P(('dom', 'tool')), may hold values from 0 to 127, all different within a row; in each aligned block of 64 rows (0 to 63, 64 to 127, ...) at most 2 rows name the same one
- local_seg: int32 [8192, 2], P(('dom', 'tool')), may hold values from 0 to 255
- active: int32 [8192, 64], P(('dom', 'tool')), may hold values 0 or 1
- stiffness: float32 [8192, 5, 4096], P(('dom', 'tool')), may hold values from -0.3125 to 0.3125
- columns: int32 [8192, 5], P(('dom', 'tool')), may hold values from 0 to 67, as said below
- vectors: float32 [8192, 4096], P(('dom', 'tool')), may hold values from -6 to 6
Outputs:
- product: float32 [8192, 4096], P(('dom', 'tool'))
The draws below stay inside these ranges and needn't reach their ends.
Inputs may be any that keep to these rules, and one draw needn't show every extreme that they name: Among the 64 node blocks of one device no owner is named by more than 2 candidates, a bound that some block reaches; a block's candidates name different owners. `columns`: the first column of each row is the row's own block, column 2 + b mod 64; the others lie within 2 blocks of it.
All inputs are finite; a program needn't handle non-finite values. No bound on the sum of `active` on one device may be relied on, other than what follows from the above.
Results may differ from the reference program's by a relative error of at most 0.0003.
Values sent between devices are 32-bit elements; how exact they have to be, the bound alone decides.
A program may use at most 128 MiB of HBM per device.

```python
import math
import jax
import jax.numpy as jnp
import numpy as np
from jax import lax

NODE = 64
NVEC = 64
FIELDS = 8
CAND = 2
NNZ = 5
HB = 2
BLK_DEV = 64
SEG_DEV = 256
CAP = 2
BLOCKS = 8192
SEGS = 32768
N_DOM = 16
N_TOOL = 8


def draw_columns(key, part):
    local_row = jnp.arange(BLOCKS, dtype=jnp.int32) % BLK_DEV
    offsets = jax.random.randint(key, (BLOCKS, NNZ), -HB, HB + 1).astype(jnp.int32)
    offsets = offsets.at[:, 0].set(0)
    return local_row[:, None] + HB + offsets


def set_ends(values, rng, low, top_value):
    extent = values.shape
    spot = [jax.random.randint(jax.random.fold_in(rng, axis), (), 0, extent[axis]) for axis in range(len(extent))]
    values = values.at[tuple(spot)].set(low)
    longest = extent.index(max(extent))
    spot[longest] = (spot[longest] + 1) % extent[longest]
    return values.at[tuple(spot)].set(top_value)


def block_levels(key, extent, split, low, top_value):
    def one(axis_at, blocks):
        draws = jax.random.uniform(jax.random.fold_in(jax.random.fold_in(key, 6), axis_at), (blocks,), jnp.float32, low / len(split), top_value / len(split))
        return jnp.repeat(jnp.exp(draws), extent[axis_at] // blocks).reshape((-1,) + (1,) * (len(extent) - axis_at - 1))

    level = one(*split[0])
    for cut in split[1:]:
        level = level * one(*cut)
    return level


def routed_block(rng, own, number, rows, number_of, top, reach, skew):
    sequence = jax.random.permutation(rng, number_of)
    heavy_load, ordinary = load_shares(number_of, rows * top, reach, skew, True), load_shares(number_of, rows * top, reach, skew, False)
    places = jnp.arange(number_of)

    def named(lengths, turn):
        used = int((lengths > 0).sum())
        fixed = max(1, used // 4)
        passed = fixed + (places - fixed + turn * (used - fixed)) % max(1, number_of - fixed)
        return jnp.zeros((number_of,), jnp.int32).at[sequence[jnp.where(places < fixed, places, passed)]].set(jnp.asarray(lengths, jnp.int32))

    lengths = jnp.where(number % 4 == 0, named(heavy_load, number // 4), named(ordinary, number - number // 4 - 1))
    mixed = jax.random.permutation(jax.random.fold_in(own, 3), number_of)
    source_of, taker = mixed[0:number_of // 2 * 2:2], mixed[1:number_of // 2 * 2:2]
    margin = jnp.minimum(lengths[source_of] - 1, reach - lengths[taker]) // 2
    margin = jnp.where((source_of == sequence[0]) | (taker == sequence[0]) | (lengths[taker] == 0), 0, jnp.maximum(margin, 0))
    passed = jax.random.randint(jax.random.fold_in(own, 4), (number_of // 2,), 0, 1 << 20) % (margin + 1)
    lengths = lengths.at[source_of].add(-passed).at[taker].add(passed)
    members = jnp.searchsorted(jnp.cumsum(lengths), jnp.arange(rows * top), side="right").astype(jnp.int32)
    grid = members.reshape(top, rows).T
    grid = grid[jax.random.permutation(jax.random.fold_in(own, 1), rows)]
    turn = jax.random.randint(jax.random.fold_in(own, 2), (rows, 1), 0, top)
    return jnp.take_along_axis(grid, (jnp.arange(top)[None, :] + turn) % top, axis=1)


def load_shares(amount, total, most, lean, full):
    loads = [(1 << 20) // math.isqrt(rank ** lean) + 1 for rank in range(1, amount + 1)]
    largest = most if full else min(most, max(-(-total // amount), total * loads[0] // sum(loads)))
    least = 1 if total - largest >= amount - 1 else 0
    counts, surplus = [largest] + [least] * (amount - 1), total - largest - least * (amount - 1)
    while surplus > 0:
        candidates = [i for i in range(1, amount) if counts[i] < largest] or [i for i in range(1, amount) if counts[i] < most]
        whole, left = sum([loads[i] for i in candidates]), surplus
        for i in candidates:
            more = min(most - counts[i], max(1, left * loads[i] // whole), surplus)
            counts[i] = counts[i] + more
            surplus = surplus - more
    return np.array(counts)


def scatter_about(own_key, extent, scale, bound, split=(), kind=jnp.bfloat16):
    values = jax.random.normal(own_key, extent, jnp.float32) * scale
    if len(split) > 0:
        values = block_levels(own_key, extent, split, -0.22, 0.18) * values
    return jnp.clip(values, min=-bound, max=bound).astype(kind)


def setup_inputs(seed: int = 0) -> dict:
    key_list = jax.random.split(jax.random.key(seed), 9)
    records = scatter_about(key_list[0], (BLOCKS, FIELDS * NODE), 1.0, 6.0, ((0, 128),), jnp.float32)
    tool_data = scatter_about(key_list[1], (SEGS, FIELDS * NODE), 1.0, 6.0, ((0, 128),), jnp.float32)
    owners_keys = jax.random.split(jax.random.fold_in(key_list[2], 1), BLOCKS // BLK_DEV)
    owners_turns = jax.random.permutation(jax.random.fold_in(key_list[2], 3), BLOCKS // BLK_DEV)
    owners = jax.vmap(lambda own, number: routed_block(jax.random.fold_in(key_list[2], 2), own, number, BLK_DEV, N_DOM * N_TOOL, CAND, CAP, 2))(owners_keys, owners_turns).reshape((BLOCKS, CAND))
    local_seg = set_ends(jax.random.randint(key_list[3], (BLOCKS, CAND), 0, SEG_DEV), jax.random.fold_in(key_list[3], 1), 0, SEG_DEV - 1).astype(jnp.int32)
    active = set_ends((jax.random.randint(key_list[4], (BLOCKS, NODE), 0, 4) < 3).astype(jnp.int32), jax.random.fold_in(key_list[4], 1), 0, 1)
    stiffness = scatter_about(key_list[5], (BLOCKS, NNZ, NODE * NODE), (NODE * NNZ) ** -0.5, 0.3125, ((0, 128),), jnp.float32)
    columns = draw_columns(jax.random.fold_in(key_list[8], 71), 0)
    vectors = scatter_about(key_list[7], (BLOCKS, NODE * NVEC), 1.0, 6.0, ((0, 128),), jnp.float32)
    return dict(records=records, tool_data=tool_data, owners=owners, local_seg=local_seg, active=active, stiffness=stiffness, columns=columns, vectors=vectors)


def mortar_tiles(part_rec, tool_rec):
    part = part_rec.reshape(part_rec.shape[:-1] + (FIELDS, NODE))
    tool = tool_rec.reshape(tool_rec.shape[:-1] + (FIELDS, NODE))
    apart = part[..., 0:3, :, None] - tool[..., 0:3, None, :]
    distance = jnp.sum(apart * apart, axis=-3)
    aligned = jnp.sum(part[..., 3:6, :, None] * tool[..., 3:6, None, :], axis=-3)
    phase = 3.0 * aligned + part[..., 6, :, None] * tool[..., 6, None, :]
    sliding = 1.0 + 0.5 * jnp.tanh(part[..., 7, :, None] * tool[..., 7, None, :])
    return jnp.exp(-distance / 8.0) * jnp.cos(phase) * sliding


def reference(records, tool_data, owners, local_seg, active, stiffness, columns, vectors):
    devices = N_DOM * N_TOOL
    hp = lax.Precision.HIGHEST
    vec_blocks = vectors.reshape(BLOCKS, NODE, NVEC)
    rim_zeros = jnp.zeros((HB, NODE, NVEC), jnp.float32)
    padded = jnp.concatenate([rim_zeros, vec_blocks, rim_zeros], axis=0)

    def one_device(device):
        start = (device * BLK_DEV).astype(jnp.int32)
        part_rows = lax.dynamic_slice_in_dim(records, start, BLK_DEV, 0)
        owner_ids = lax.dynamic_slice_in_dim(owners, start, BLK_DEV, 0)
        seg_local = lax.dynamic_slice_in_dim(local_seg, start, BLK_DEV, 0)
        flags = lax.dynamic_slice_in_dim(active, start, BLK_DEV, 0).astype(jnp.float32)[:, :, None]
        blocks_here = lax.dynamic_slice_in_dim(stiffness, start, BLK_DEV, 0).reshape(BLK_DEV, NNZ, NODE, NODE)
        column_ids = lax.dynamic_slice_in_dim(columns, start, BLK_DEV, 0)
        segment = (owner_ids * SEG_DEV + seg_local).astype(jnp.int32)
        tiles = mortar_tiles(part_rows[:, None, :], tool_data[segment])
        local_vec = lax.dynamic_slice_in_dim(vec_blocks, start, BLK_DEV, 0)
        masked = flags * local_vec
        inward = jnp.einsum('bkij,biv->bkjv', tiles, masked, precision=hp)
        outward = jnp.einsum('bkij,bkjv->biv', tiles, inward, precision=hp)
        contact = 0.05 * flags * outward
        extended = lax.dynamic_slice_in_dim(padded, start, BLK_DEV + 2 * HB, 0)
        nearby = extended[column_ids]
        inner = jnp.einsum('bkij,bkjv->biv', blocks_here, nearby, precision=hp)
        return (inner + contact).reshape(BLK_DEV, NODE * NVEC)

    result = lax.map(one_device, jnp.arange(devices, dtype=jnp.int32))
    return result.reshape(BLOCKS, NODE * NVEC)
```

```python
import math
import jax
import jax.numpy as jnp
import numpy as np
from jax import lax
from jax.experimental import pallas as pl
from jax.experimental.pallas import tpu as pltpu
from jax.sharding import PartitionSpec as P
F32, BF16 = jnp.float32, jnp.bfloat16
NB, HB, E5 = 64, 2, 5
ALPHA = math.sqrt(math.log2(math.e) / 8.0)
TURN = 1.0 / (2.0 * math.pi)
def fit():
    r = np.cos(np.linspace(0, np.pi / 2, 4001))[:-1] * 0.5
    n = 6
    w = np.sqrt(2.0) * np.sin(np.pi * r) / r
    A = np.stack([r ** (2 * k) for k in range(n)], 1)
    c = np.linalg.lstsq(A * r[:, None], w * r, rcond=None)[0]
    return [float(x) for x in c], np.abs((A @ c - w) * r).max()
SINC, SERR = fit()

def split(x):
    hi = x.astype(BF16)
    return hi, (x - hi.astype(F32)).astype(BF16)

def to_w(src, dst, row0):
    for t in range(32):
        dst[pl.ds(row0 + t, 8, stride=32), :] = src[:, t * 128:(t + 1) * 128]

def prep_vec(vw, nat, bv, vt, c, own):
    lane = lax.broadcasted_iota(jnp.int32, (32, 128), 1)
    w = vw[pl.ds(pl.multiple_of(c * 32, 32), 32), :]
    wr = pltpu.roll(w, 64, 1)
    nat[pl.ds(0, 32, stride=2), :] = jnp.where(lane < 64, w, wr)
    nat[pl.ds(1, 32, stride=2), :] = jnp.where(lane < 64, wr, w)
    d = nat[...]
    lane2 = lax.broadcasted_iota(jnp.int32, (64, 128), 1)
    th, tl = split(jnp.where(lane2 < 64, d, 0.0))
    bh, bl = split(jnp.where(lane2 >= 64, d, 0.0))
    bv[c] = jnp.concatenate([jnp.concatenate([th, tl], 1), jnp.concatenate([bh, bl], 1)], 0)
    if own:
        vp = jnp.concatenate([w[:, :64], w[:, 64:]], 0)
        t = vp.T
        h, l = split(t)
        vt[c - HB] = jnp.concatenate([h, l], 0)

def prep_part(rec, act, rt, pb):
    rt[0:512, 0:64] = rec[...].T
    rt[512:576, 0:64] = act[...].astype(F32).T
    scale = (ALPHA,) * 3 + (3.0 * TURN,) * 3 + (TURN, 1.0, 1.0)
    def group(g, carry):
        for f in range(9):
            x = jnp.concatenate([rt[pl.ds(f * 64, 32, stride=2), :], rt[pl.ds(f * 64 + 1, 32, stride=2), :]], 0) * scale[f]
            x = pltpu.roll(x, 128 - g * 8, 1)
            for k in range(8):
                pb[g * 8 + k, f] = jnp.broadcast_to(x[:, k:k + 1], (64, 128))
        return carry
    lax.fori_loop(0, 8, group, 0)

def inner_block(cols, sw, bv, iw, b, bb):
    w = jnp.concatenate([sw[e, bb * 32:(bb + 1) * 32, :] for e in range(E5)], 1)
    h, l = split(w)
    r = jnp.concatenate([bv[cols[e, b]] for e in range(E5)], 0)
    o = jnp.dot(jnp.concatenate([h, l], 0), r, preferred_element_type=F32)
    iw[pl.ds(pl.multiple_of(b * 32, 32), 32), :] = (o[:32, :128] + o[:32, 128:]) + (o[32:, :128] + o[32:, 128:])

def cand_rows(got, s):
    x = got[s // 2]
    return jnp.where(lax.rem(s, 2) == 1, x[4:8], x[0:4])

def contact_block(slot, got, pb, vt, b):
    lane = lax.broadcasted_iota(jnp.int32, (4, 128), 1)
    sub = lax.broadcasted_iota(jnp.int32, (4, 128), 0)
    g0, g1 = cand_rows(got, slot[0, b]), cand_rows(got, slot[0, 64 + b])
    ev = jnp.where(lane < 64, g0, pltpu.roll(g1, 64, 1)) * jnp.where(sub < 2, ALPHA, 1.0)
    od = jnp.where(lane < 64, pltpu.roll(g0, 64, 1), g1) * jnp.where(sub < 1, ALPHA, 1.0)
    q = (ev[0:1], od[0:1], ev[1:2])
    m = (od[1:2], ev[2:3], od[2:3])
    thick, fric = ev[3:4], od[3:4]
    dist = sum((pb[b, f] - q[f]) ** 2 for f in range(3))
    x = sum(pb[b, 3 + f] * m[f] for f in range(3)) + pb[b, 6] * thick
    r = x - jnp.round(x)
    r2 = r * r
    s = SINC[5]
    for c in SINC[4::-1]:
        s = s * r2 + c
    s = s * r
    tile = jnp.exp2(-dist) * (1.0 - s * s) * ((jnp.tanh(pb[b, 7] * fric) * 0.5 + 1.0) * pb[b, 8])
    th, tl = split(tile)
    y = jnp.dot(vt[b], jnp.concatenate([th, tl], 1), preferred_element_type=F32)
    inw = (y[:64, :128] + y[:64, 128:]) + (y[64:, :128] + y[64:, 128:])
    ih, il = split(inw)
    o = lax.dot_general(jnp.concatenate([th, tl], 0), jnp.concatenate([ih, il], 0), (((1,), (1,)), ((), ())), preferred_element_type=F32)
    a = o[:64] + o[64:]
    ae, ao = a[:32], a[32:]
    l2 = lax.broadcasted_iota(jnp.int32, (32, 128), 1)
    return jnp.where(l2 < 64, ae, ao) + pltpu.roll(jnp.where(l2 < 64, ao, ae), 64, 1)

MESH = pl.DeviceIdType.MESH
N = 128


def peer(j):
    me = lax.axis_index("dom") * 8 + lax.axis_index("tool")
    d = lax.rem(me + j, N)
    return d, (d // 8, lax.rem(d, 8)), me


def exchange(own_ref, seg_ref, tool_ref, vec, got, slot_ref, lo, hi, req_s, req_r, resp, ss1, rs1, ss2, rs2, hs, hr):
    barrier = pltpu.get_barrier_semaphore()

    def sig(j, c):
        d, where, me = peer(j)
        pl.semaphore_signal(barrier, inc=1, device_id=where, device_id_type=MESH)
        return c

    lax.fori_loop(1, N, sig, 0)
    own = jnp.concatenate([own_ref[0:1, :], own_ref[1:2, :]], axis=1)
    seg = jnp.concatenate([seg_ref[0:1, :], seg_ref[1:2, :]], axis=1)
    row = lax.broadcasted_iota(jnp.int32, (N, N), 0)
    col = lax.broadcasted_iota(jnp.int32, (N, N), 1)
    hit = jnp.broadcast_to(own, (N, N)) == row
    key = jnp.broadcast_to(col[0:1] * 256 + seg, (N, N))
    kmin = jnp.min(jnp.where(hit, key, 1 << 20), axis=1, keepdims=True)
    kmax = jnp.max(jnp.where(hit, key, 0), axis=1, keepdims=True)
    req_s[...] = (jnp.where(col == 0, kmin, kmax) & 255).reshape(N, 1, N)
    slot_ref[...] = own * 2 + jnp.sum(jnp.where(hit & (key != kmin), 1, 0), axis=0, keepdims=True)
    pl.semaphore_wait(barrier, N - 1)
    me = lax.axis_index("dom") * 8 + lax.axis_index("tool")
    nxt, after, _ = peer(1)
    prv, before, _ = peer(N - 1)
    down = pltpu.make_async_remote_copy(vec.at[pl.ds(56, 8)], lo, hs.at[0], hr.at[0], device_id=after, device_id_type=MESH)
    up = pltpu.make_async_remote_copy(vec.at[pl.ds(0, 8)], hi, hs.at[1], hr.at[1], device_id=before, device_id_type=MESH)
    pltpu.make_async_copy(req_s.at[me], req_r.at[me], rs1).start()

    def send(j, c):
        d, where, me = peer(j)
        pltpu.make_async_remote_copy(req_s.at[d], req_r.at[me], ss1, rs1, device_id=where, device_id_type=MESH).start()
        return c

    lax.fori_loop(1, N, send, 0)
    down.start()
    up.start()
    pltpu.make_async_copy(req_r, req_r, rs1).wait()
    ask = req_r[...].reshape(N, N)
    for r in range(2):
        hot = (lax.broadcasted_iota(jnp.int32, (N, 256), 1) == ask[:, r:r + 1]).astype(jnp.float32)
        g = jnp.dot(hot, tool_ref[...], precision=lax.Precision.HIGHEST, preferred_element_type=jnp.float32)
        for f in range(4):
            resp[:, r * 4 + f, :] = g[:, f * 128:(f + 1) * 128]
    pltpu.make_async_copy(req_s.at[pl.ds(0, N - 1)], req_s.at[pl.ds(0, N - 1)], ss1).wait()
    pltpu.make_async_copy(resp.at[me], got.at[me], rs2).start()

    def reply(j, c):
        d, where, me = peer(j)
        pltpu.make_async_remote_copy(resp.at[d], got.at[me], ss2, rs2, device_id=where, device_id_type=MESH).start()
        return c

    lax.fori_loop(1, N, reply, 0)
    down.wait()
    up.wait()

    @pl.when(me == 0)
    def _():
        lo[...] = jnp.zeros_like(lo)

    @pl.when(me == N - 1)
    def _():
        hi[...] = jnp.zeros_like(hi)

    pltpu.make_async_copy(got, got, rs2).wait()
    pltpu.make_async_copy(resp.at[pl.ds(0, N - 1)], resp.at[pl.ds(0, N - 1)], ss2).wait()

def body(slot, cols, got, rec, act, s_hbm, vec, lo, hi, out, s_v, sw, vw, nat, bv, vt, rt, pb, iw, sems):
    def cp(g): return pltpu.make_async_copy(s_hbm.at[:, pl.ds(pl.multiple_of(g*8,8),8), :], s_v.at[:, pl.ds(pl.multiple_of(g*8,8),8), :], sems.at[g])
    for g in range(8): cp(g).start()
    to_w(lo, vw, 0); to_w(hi, vw, 256+2048)
    def tw(g, c):
        to_w(vec[pl.ds(pl.multiple_of(g*8,8),8),:], vw, 256+g*256); return c
    lax.fori_loop(0,8,tw,0)
    vww = vw.at[pl.ds(192, 68*32)]
    for c in (0,1,66,67): prep_vec(vww, nat, bv, vt, c, False)
    def pv(c, k): prep_vec(vww, nat, bv, vt, c, True); return k
    lax.fori_loop(2,66,pv,0)
    prep_part(rec, act, rt, pb)
    def ig(g, c):
        cp(g).wait()
        for e in range(E5): to_w(s_v[e, pl.ds(pl.multiple_of(g*8,8),8), :], sw.at[e], 0)
        for bb in range(8): inner_block(cols, sw, bv, iw, g*8+bb, bb)
        return c
    lax.fori_loop(0,8,ig,0)
    def cg(b, c):
        z = contact_block(slot, got, pb, vt, b)
        iw[pl.ds(pl.multiple_of(b*32,32),32),:] = iw[pl.ds(pl.multiple_of(b*32,32),32),:] + 0.05*z
        return c
    lax.fori_loop(0,64,cg,0)
    def og(g, c):
        for t in range(32):
            out[pl.ds(pl.multiple_of(g*8,8),8), t*128:(t+1)*128] = iw[pl.ds(g*256+t, 8, stride=32), :]
        return c
    lax.fori_loop(0,8,og,0)

V = pl.BlockSpec(memory_space=pltpu.VMEM)
S = pl.BlockSpec(memory_space=pltpu.SMEM)
A = pl.BlockSpec(memory_space=pl.ANY)


def per_device(records, tool_data, owners, local_seg, active, stiffness, columns, vectors):
    got, slot, lo, hi = pl.pallas_call(
        exchange,
        out_shape=(jax.ShapeDtypeStruct((N, 8, 128), F32), jax.ShapeDtypeStruct((1, N), jnp.int32),
                   jax.ShapeDtypeStruct((8, 4096), F32), jax.ShapeDtypeStruct((8, 4096), F32)),
        in_specs=[V, V, V, A], out_specs=(V, V, V, V),
        scratch_shapes=[pltpu.VMEM((N, 1, N), jnp.int32), pltpu.VMEM((N, 1, N), jnp.int32), pltpu.VMEM((N, 8, 128), F32)]
        + [pltpu.SemaphoreType.DMA] * 4 + [pltpu.SemaphoreType.DMA((2,))] * 2,
        compiler_params=pltpu.CompilerParams(collective_id=0, has_side_effects=True, vmem_limit_bytes=40 << 20),
        name="exchange",
    )(owners.T, local_seg.T, tool_data, vectors)
    return pl.pallas_call(
        body, out_shape=jax.ShapeDtypeStruct((NB, 4096), F32),
        in_specs=[S, S, V, V, V, A, V, V, V], out_specs=V,
        scratch_shapes=[pltpu.VMEM((5, 64, 4096), F32), pltpu.VMEM((5, 256, 128), F32), pltpu.VMEM((80 * 32, 128), F32),
                        pltpu.VMEM((64, 128), F32), pltpu.VMEM((68, 128, 256), BF16), pltpu.VMEM((64, 128, 64), BF16),
                        pltpu.VMEM((576, 128), F32), pltpu.VMEM((64, 9, 64, 128), F32), pltpu.VMEM((2048, 128), F32),
                        pltpu.SemaphoreType.DMA((8,))],
        compiler_params=pltpu.CompilerParams(vmem_limit_bytes=60 << 20), name="mortar",
    )(slot, columns.T, got, records, active, stiffness.transpose(1, 0, 2), vectors, lo, hi)


def solution(mesh):
    ax = P(("dom", "tool"), None)
    return jax.shard_map(per_device, mesh=mesh, in_specs=(ax,) * 5 + (P(("dom", "tool"), None, None), ax, ax), out_specs=ax, check_vma=False)
```

```python
import math
import jax
import jax.numpy as jnp
import numpy as np
from jax import lax
from jax.experimental import pallas as pl
from jax.experimental.pallas import tpu as pltpu
from jax.sharding import PartitionSpec as P
F32, BF16 = jnp.float32, jnp.bfloat16
NB, HB, E5 = 64, 2, 5
A2 = math.log2(math.e) / 8.0
TURN = 1.0 / (2.0 * math.pi)
def fit():
    r = np.cos(np.linspace(0, np.pi / 2, 4001))[:-1] * 0.5
    w = np.sqrt(2.0) * np.sin(np.pi * r) / r
    a = np.stack([r ** (2 * k) for k in range(5)], 1)
    c = np.linalg.lstsq(a * r[:, None], w * r, rcond=None)[0]
    return [float(x) for x in c]


SINC = fit()

def iota(shape, dim):
    return lax.broadcasted_iota(jnp.int32, shape, dim)

def split(x):
    hi = x.astype(BF16)
    return hi, (x - hi.astype(F32)).astype(BF16)

def split3(x):
    h = x.astype(BF16).astype(F32)
    y = x - h
    m = y.astype(BF16).astype(F32)
    return h, m, y - m

def to_w(src, dst, row0):
    for t in range(32):
        dst[pl.ds(row0 + t, 8, stride=32), :] = src[:, t * 128:(t + 1) * 128]

def pair8(g0, g1):
    lane = iota((4, 128), 1)
    ev = jnp.where(lane < 64, g0, pltpu.roll(g1, 64, 1))
    od = jnp.where(lane < 64, pltpu.roll(g0, 64, 1), g1)
    return jnp.concatenate([ev, od], 0)

def mask_rows(which):
    s = iota((8, 128), 0)
    m = s == which[0]
    for w in which[1:]:
        m = m | (s == w)
    return m

def square_sum(x):
    return jnp.sum(jnp.where(mask_rows((0, 1, 4)), x * x, 0.0), 0, keepdims=True) * A2

def prep_vec(vw, nat, bv, c, own_b, vt, dw):
    w = vw[pl.ds(pl.multiple_of(c * 32, 32), 32), :]
    lane = iota((32, 128), 1)
    wr = pltpu.roll(w, 64, 1)
    nat[pl.ds(0, 32, stride=2), :] = jnp.where(lane < 64, w, wr)
    nat[pl.ds(1, 32, stride=2), :] = jnp.where(lane < 64, wr, w)
    d = nat[...]
    lane2 = iota((64, 128), 1)
    h, l = split(d)
    z = jnp.zeros_like(h)
    lo, up = lane2 < 64, lane2 >= 64
    bv[c] = jnp.concatenate([jnp.concatenate([jnp.where(lo, h, z), jnp.where(lo, l, z)], 1),
                             jnp.concatenate([jnp.where(up, h, z), jnp.where(up, l, z)], 1)], 0)
    if own_b is not None:
        w = w * dw[own_b]
        t = jnp.concatenate([w[:, :64], w[:, 64:]], 0).T
        h, l = split(t)
        vt[own_b] = jnp.concatenate([h, h, l], 1)

def prep_act(act, at, dw):
    at[...] = act[...].astype(F32).T
    a = jnp.concatenate([at[pl.ds(0, 32, stride=2), :], at[pl.ds(1, 32, stride=2), :]], 1).astype(BF16)
    row, col = iota((128, 128), 0), iota((128, 128), 1)
    same = (row // 64) == (col // 64)
    def one(g, carry):
        for k in range(4):
            b = g * 4 + k
            hot = jnp.where(same & (lax.rem(row, 64) == b), 1.0, 0.0).astype(BF16)
            dw[b] = jnp.dot(a, hot, preferred_element_type=F32)
        return carry
    lax.fori_loop(0, 16, one, 0)

def prep_part(rw, ft, lhs, g, k):
    r4 = rw[pl.ds(pl.multiple_of(g * 8, 8), 8), :]
    p = pair8(r4[0:4], r4[4:8])
    sub = iota((8, 128), 0)
    pos = mask_rows((0, 1, 4))
    ph, pm, pl_ = split3(-square_sum(p))
    extra = jnp.where(sub < 3, -1.0, jnp.where(sub == 3, ph, jnp.where(sub == 4, pm, jnp.where(sub == 5, pl_, 0.0))))
    scale = jnp.where(pos, 2.0 * A2, jnp.where(sub == 7, 1.0, jnp.where(sub == 3, TURN, 3.0 * TURN)))
    h, m, l = split3(p * scale)
    zero = jnp.zeros_like(h)
    for n, mk in enumerate((pos, mask_rows((2, 3, 5, 6)), sub == 7)):
        hh, mm, ll = (jnp.where(mk, x, 0.0) for x in (h, m, l))
        f = jnp.concatenate([hh, hh, hh, mm, mm, ll, extra if n == 0 else zero, zero], 0)
        ft[n, k] = f.T
    for q in range(2):
        parts = []
        for n in range(3):
            for par in range(2):
                parts.append(ft[n, k, pl.ds(q * 64 + par, 32, stride=2), :])
        lhs[g * 2 + q] = jnp.concatenate(parts, 0).astype(BF16)

def inner_block(cols, sw, bv, iw, b, bb):
    w = jnp.concatenate([sw[e, bb * 32:(bb + 1) * 32, :] for e in range(E5)], 1)
    h, l = split(w)
    r = jnp.concatenate([bv[cols[e, b]] for e in range(E5)], 0)
    o = jnp.dot(jnp.concatenate([h, l], 0), r, preferred_element_type=F32)
    iw[pl.ds(pl.multiple_of(b * 32, 32), 32), :] = (o[:32, :128] + o[:32, 128:]) + (o[32:, :128] + o[32:, 128:])

def cand_rows(got, s):
    x = got[s // 2]
    return jnp.where(lax.rem(s, 2) == 1, x[4:8], x[0:4])

def tile_of(slot, got, lhs, b):
    x = pair8(cand_rows(got, slot[0, b]), cand_rows(got, slot[0, 64 + b]))
    sub = iota((8, 128), 0)
    h, m, l = split3(x)
    qh, qm, ql = split3(square_sum(x))
    extra = jnp.where(sub == 0, qh, jnp.where(sub == 1, qm, jnp.where(sub == 2, ql, jnp.where(sub < 6, 1.0, 0.0))))
    rhs = jnp.concatenate([h, m, l, h, m, h, extra, jnp.zeros_like(h)], 0).astype(BF16)
    z = jnp.dot(lhs[b], rhs, preferred_element_type=F32)
    x = z[64:128]
    r = x - jnp.round(x)
    r2 = r * r
    s = SINC[4]
    for c in SINC[3::-1]:
        s = s * r2 + c
    s = s * r
    tile = jnp.exp2(z[:64]) * (1.0 - s * s) * (jnp.tanh(z[128:]) * 0.5 + 1.0)
    return split(tile)

def first(vt, b, th, tl):
    y = jnp.dot(vt[b], jnp.concatenate([th, tl, th], 0), preferred_element_type=F32)
    return split(y)

def second(dw, b, th, tl, ih, il):
    o = lax.dot_general(jnp.concatenate([th, th, tl], 1), jnp.concatenate([ih, il, ih], 1), (((1,), (1,)), ((), ())), preferred_element_type=F32)
    return jnp.concatenate([o[:32], o[32:]], 1) * (dw[b] * 0.05)

MESH = pl.DeviceIdType.MESH
N = 128
UC = 8


def peer(j):
    me = lax.axis_index("dom") * 8 + lax.axis_index("tool")
    d = lax.rem(me + j, N)
    return d, (d // 8, lax.rem(d, 8)), me


def rows8(g):
    return pl.ds(pl.multiple_of(g * 8, 8), 8)


def local(src, dst, sem):
    return pltpu.make_async_copy(src, dst, sem)


def kernel(own_h, seg_h, tool_h, vec_h, cols_h, rec_h, act_h, s_h, out,
           own_v, seg_v, tool, vec, cols, rec, act, s_v, slot_v, slot,
           req_s, req_r, resp, got, lo, hi,
           sw, vw, nat, bv, vt, at, dw, rw, ft, lhs, iw,
           ls, gs, ss1, rs1, ss2, rs2, hs, hr):
    loads = [local(a, b, ls.at[i]) for i, (a, b) in enumerate(
        ((own_h, own_v), (seg_h, seg_v), (tool_h, tool), (vec_h, vec), (cols_h, cols), (rec_h, rec), (act_h, act)))]
    for c in loads:
        c.start()

    def stiff(g):
        return local(s_h.at[:, rows8(g), :], s_v.at[:, rows8(g), :], gs.at[g])

    for g in range(8):
        stiff(g).start()
    barrier = pltpu.get_barrier_semaphore()

    def sig(j, c):
        d, where, me = peer(j)
        pl.semaphore_signal(barrier, inc=1, device_id=where, device_id_type=MESH)
        return c

    lax.fori_loop(1, N, sig, 0)
    loads[0].wait()
    loads[1].wait()
    own = jnp.concatenate([own_v[0:1, :], own_v[1:2, :]], axis=1)
    seg = jnp.concatenate([seg_v[0:1, :], seg_v[1:2, :]], axis=1)
    row, col = iota((N, N), 0), iota((N, N), 1)
    hit = jnp.broadcast_to(own, (N, N)) == row
    key = jnp.broadcast_to(col[0:1] * 256 + seg, (N, N))
    kmin = jnp.min(jnp.where(hit, key, 1 << 20), axis=1, keepdims=True)
    kmax = jnp.max(jnp.where(hit, key, 0), axis=1, keepdims=True)
    req_s[...] = (jnp.where(col == 0, kmin, kmax) & 255).reshape(N, 1, N)
    slot_v[...] = own * 2 + jnp.sum(jnp.where(hit & (key != kmin), 1, 0), axis=0, keepdims=True)
    pl.semaphore_wait(barrier, N - 1)
    me = lax.axis_index("dom") * 8 + lax.axis_index("tool")
    _, after, _ = peer(1)
    _, before, _ = peer(N - 1)
    down = pltpu.make_async_remote_copy(vec_h.at[pl.ds(56, 8)], lo, hs.at[0], hr.at[0], device_id=after, device_id_type=MESH)
    up = pltpu.make_async_remote_copy(vec_h.at[pl.ds(0, 8)], hi, hs.at[1], hr.at[1], device_id=before, device_id_type=MESH)
    local(req_s.at[me], req_r.at[me], rs1).start()

    def send(j, c):
        d, where, me = peer(j)
        pltpu.make_async_remote_copy(req_s.at[d], req_r.at[me], ss1, rs1, device_id=where, device_id_type=MESH).start()
        return c

    lax.fori_loop(1, N, send, 0)
    down.start()
    up.start()
    keep = local(slot_v, slot, ls.at[7])
    keep.start()
    loads[3].wait()
    loads[6].wait()
    prep_act(act, at, dw)
    vww = vw.at[pl.ds(192, 68 * 32)]

    def relay(g, c):
        to_w(vec[rows8(g), :], vw, 256 + g * 256)
        return c

    lax.fori_loop(0, 8, relay, 0)

    def pv(g, c):
        for u in range(4):
            prep_vec(vww, nat.at[u], bv, g * 4 + u + 2, g * 4 + u, vt, dw)
        return c

    lax.fori_loop(0, 16, pv, 0)
    loads[2].wait()
    local(req_r, req_r, rs1).wait()
    ask = req_r[...].reshape(N, N)
    for r in range(2):
        hot = (iota((N, 256), 1) == ask[:, r:r + 1]).astype(F32)
        g = jnp.dot(hot, tool[...], precision=lax.Precision.HIGHEST, preferred_element_type=F32)
        for f in range(4):
            resp[:, r * 4 + f, :] = g[:, f * 128:(f + 1) * 128]
    local(resp.at[me], got.at[me], rs2).start()

    def reply(j, c):
        d, where, me = peer(j)
        pltpu.make_async_remote_copy(resp.at[d], got.at[me], ss2, rs2, device_id=where, device_id_type=MESH).start()
        return c

    lax.fori_loop(1, N, reply, 0)
    down.wait()
    up.wait()

    @pl.when(me == 0)
    def _():
        lo[...] = jnp.zeros_like(lo)

    @pl.when(me == N - 1)
    def _():
        hi[...] = jnp.zeros_like(hi)

    to_w(lo, vw, 0)
    to_w(hi, vw, 256 + 2048)
    for i, c in enumerate((0, 1, 66, 67)):
        prep_vec(vww, nat.at[i], bv, c, None, vt, dw)
    loads[5].wait()
    for b0 in range(8):
        for f in range(4):
            rw[pl.ds(b0 * 32 + f, 8, stride=4), :] = rec[b0 * 8:b0 * 8 + 8, f * 128:(f + 1) * 128]

    def pp(g, c):
        for u in range(2):
            prep_part(rw, ft, lhs, g * 2 + u, u)
        return c

    lax.fori_loop(0, 16, pp, 0)
    loads[4].wait()

    def ig(g, c):
        stiff(g).wait()
        for e in range(E5):
            to_w(s_v[e, rows8(g), :], sw.at[e], 0)
        for bb in range(8):
            inner_block(cols, sw, bv, iw, g * 8 + bb, bb)
        return c

    lax.fori_loop(0, 8, ig, 0)
    keep.wait()
    local(req_s.at[pl.ds(0, N - 1)], req_s.at[pl.ds(0, N - 1)], ss1).wait()
    local(got, got, rs2).wait()

    def cg(g, c):
        bs = [g * UC + u for u in range(UC)]
        t = [tile_of(slot, got, lhs, b) for b in bs]
        y = [first(vt, b, *x) for b, x in zip(bs, t)]
        z = [second(dw, b, *x, *w) for b, x, w in zip(bs, t, y)]
        at32 = [pl.ds(pl.multiple_of(b * 32, 32), 32) for b in bs]
        total = [iw[a, :] + w for a, w in zip(at32, z)]
        for a, w in zip(at32, total):
            iw[a, :] = w
        return c

    lax.fori_loop(0, NB // UC, cg, 0)

    def og(g, c):
        for t in range(32):
            out[rows8(g), t * 128:(t + 1) * 128] = iw[pl.ds(g * 256 + t, 8, stride=32), :]
        return c

    lax.fori_loop(0, 8, og, 0)
    local(resp.at[pl.ds(0, N - 1)], resp.at[pl.ds(0, N - 1)], ss2).wait()


def per_device(records, tool_data, owners, local_seg, active, stiffness, columns, vectors):
    vm, sm, dma = pltpu.VMEM, pltpu.SMEM, pltpu.SemaphoreType.DMA
    i32 = jnp.int32
    return pl.pallas_call(
        kernel,
        out_shape=jax.ShapeDtypeStruct((NB, 4096), F32),
        in_specs=[pl.BlockSpec(memory_space=pl.ANY)] * 8,
        out_specs=pl.BlockSpec(memory_space=vm),
        scratch_shapes=[
            vm((2, NB), i32), vm((2, NB), i32), vm((256, 512), F32), vm((NB, 4096), F32), sm((E5, NB), i32),
            vm((NB, 512), F32), vm((NB, 64), i32), vm((E5, NB, 4096), F32), vm((1, N), i32), sm((1, N), i32),
            vm((N, 1, N), i32), vm((N, 1, N), i32), vm((N, 8, 128), F32), vm((N, 8, 128), F32),
            vm((8, 4096), F32), vm((8, 4096), F32),
            vm((E5, 256, 128), F32), vm((80 * 32, 128), F32), vm((4, 64, 128), F32), vm((68, 128, 256), BF16),
            vm((NB, 64, 192), BF16), vm((64, 64), F32), vm((NB, 32, 128), F32), vm((256, 128), F32),
            vm((3, 2, 128, 64), F32), vm((NB, 192, 64), BF16), vm((2048, 128), F32),
            dma((8,)), dma((8,)), dma, dma, dma, dma, dma((2,)), dma((2,)),
        ],
        compiler_params=pltpu.CompilerParams(collective_id=0, has_side_effects=True, vmem_limit_bytes=60 << 20),
        name="mortar",
    )(owners.T, local_seg.T, tool_data, vectors, columns.T, records, active, stiffness.transpose(1, 0, 2))


def solution(mesh):
    ax = P(("dom", "tool"), None)
    return jax.shard_map(per_device, mesh=mesh, in_specs=(ax,) * 5 + (P(("dom", "tool"), None, None), ax, ax), out_specs=ax, check_vma=False)
```

```python
import math
import jax
import jax.numpy as jnp
import numpy as np
from jax import lax
from jax.experimental import pallas as pl
from jax.experimental.pallas import tpu as pltpu
from jax.sharding import PartitionSpec as P
F32, BF16 = jnp.float32, jnp.bfloat16
NB, HB, E5 = 64, 2, 5
A2 = math.log2(math.e) / 8.0
TURN = 1.0 / (2.0 * math.pi)
def fit():
    r = np.cos(np.linspace(0, np.pi / 2, 4001))[:-1] * 0.5
    w = np.sqrt(2.0) * np.sin(np.pi * r) / r
    a = np.stack([r ** (2 * k) for k in range(5)], 1)
    c = np.linalg.lstsq(a * r[:, None], w * r, rcond=None)[0]
    return [float(x) for x in c]


SINC = fit()

def iota(shape, dim):
    return lax.broadcasted_iota(jnp.int32, shape, dim)

def split(x):
    hi = x.astype(BF16)
    return hi, (x - hi.astype(F32)).astype(BF16)

def split3(x):
    h = x.astype(BF16).astype(F32)
    y = x - h
    m = y.astype(BF16).astype(F32)
    return h, m, y - m

def to_w(src, dst, row0):
    for t in range(32):
        dst[pl.ds(row0 + t, 8, stride=32), :] = src[:, t * 128:(t + 1) * 128]

def pair8(g0, g1):
    lane = iota((4, 128), 1)
    ev = jnp.where(lane < 64, g0, pltpu.roll(g1, 64, 1))
    od = jnp.where(lane < 64, pltpu.roll(g0, 64, 1), g1)
    return jnp.concatenate([ev, od], 0)

def mask_rows(which):
    s = iota((8, 128), 0)
    m = s == which[0]
    for w in which[1:]:
        m = m | (s == w)
    return m

def square_sum(x):
    return jnp.sum(jnp.where(mask_rows((0, 1, 4)), x * x, 0.0), 0, keepdims=True) * A2

def prep_vec(vw, nat, bv, c, own_b, vt, dw):
    w = vw[pl.ds(pl.multiple_of(c * 32, 32), 32), :]
    lane = iota((32, 128), 1)
    wr = pltpu.roll(w, 64, 1)
    nat[pl.ds(0, 32, stride=2), :] = jnp.where(lane < 64, w, wr)
    nat[pl.ds(1, 32, stride=2), :] = jnp.where(lane < 64, wr, w)
    d = nat[...]
    lane2 = iota((64, 128), 1)
    h, l = split(d)
    z = jnp.zeros_like(h)
    lo, up = lane2 < 64, lane2 >= 64
    bv[c] = jnp.concatenate([jnp.concatenate([jnp.where(lo, h, z), jnp.where(lo, l, z)], 1),
                             jnp.concatenate([jnp.where(up, h, z), jnp.where(up, l, z)], 1)], 0)
    if own_b is not None:
        w = w * dw[own_b]
        t = jnp.concatenate([w[:, :64], w[:, 64:]], 0).T
        h, l = split(t)
        vt[own_b] = jnp.concatenate([h, h, l], 1)

def prep_act(act, at, dw):
    at[...] = act[...].astype(F32).T
    a = jnp.concatenate([at[pl.ds(0, 32, stride=2), :], at[pl.ds(1, 32, stride=2), :]], 1).astype(BF16)
    row, col = iota((128, 128), 0), iota((128, 128), 1)
    same = (row // 64) == (col // 64)
    def one(g, carry):
        for k in range(4):
            b = g * 4 + k
            hot = jnp.where(same & (lax.rem(row, 64) == b), 1.0, 0.0).astype(BF16)
            dw[b] = jnp.dot(a, hot, preferred_element_type=F32)
        return carry
    lax.fori_loop(0, 16, one, 0)

def prep_part(rw, ft, lhs, g, k):
    r4 = rw[pl.ds(pl.multiple_of(g * 8, 8), 8), :]
    p = pair8(r4[0:4], r4[4:8])
    sub = iota((8, 128), 0)
    pos = mask_rows((0, 1, 4))
    ph, pm, pl_ = split3(-square_sum(p))
    extra = jnp.where(sub < 3, -1.0, jnp.where(sub == 3, ph, jnp.where(sub == 4, pm, jnp.where(sub == 5, pl_, 0.0))))
    scale = jnp.where(pos, 2.0 * A2, jnp.where(sub == 7, 1.0, jnp.where(sub == 3, TURN, 3.0 * TURN)))
    h, m, l = split3(p * scale)
    zero = jnp.zeros_like(h)
    for n, mk in enumerate((pos, mask_rows((2, 3, 5, 6)), sub == 7)):
        hh, mm, ll = (jnp.where(mk, x, 0.0) for x in (h, m, l))
        f = jnp.concatenate([hh, hh, hh, mm, mm, ll, extra if n == 0 else zero, zero], 0)
        ft[n, k] = f.T
    for q in range(2):
        parts = []
        for n in range(3):
            for par in range(2):
                parts.append(ft[n, k, pl.ds(q * 64 + par, 32, stride=2), :])
        lhs[g * 2 + q] = jnp.concatenate(parts, 0).astype(BF16)

def inner_block(cols, sw, bv, iw, b, bb):
    w = jnp.concatenate([sw[e, bb * 32:(bb + 1) * 32, :] for e in range(E5)], 1)
    h, l = split(w)
    r = jnp.concatenate([bv[cols[e, b]] for e in range(E5)], 0)
    o = jnp.dot(jnp.concatenate([h, l], 0), r, preferred_element_type=F32)
    iw[pl.ds(pl.multiple_of(b * 32, 32), 32), :] = (o[:32, :128] + o[:32, 128:]) + (o[32:, :128] + o[32:, 128:])

def cand_rows(got, s):
    x = got[s // 2]
    return jnp.where(lax.rem(s, 2) == 1, x[4:8], x[0:4])

def tile_of(slot, got, lhs, b):
    x = pair8(cand_rows(got, slot[0, b]), cand_rows(got, slot[0, NB + b]))
    sub = iota((8, 128), 0)
    h, m, l = split3(x)
    qh, qm, ql = split3(square_sum(x))
    extra = jnp.where(sub == 0, qh, jnp.where(sub == 1, qm, jnp.where(sub == 2, ql, jnp.where(sub < 6, 1.0, 0.0))))
    rhs = jnp.concatenate([h, m, l, h, m, h, extra, jnp.zeros_like(h)], 0).astype(BF16)
    z = jnp.dot(lhs[b], rhs, preferred_element_type=F32)
    x = z[64:128]
    r = x - jnp.round(x)
    r2 = r * r
    s = SINC[4]
    for c in SINC[3::-1]:
        s = s * r2 + c
    s = s * r
    tile = jnp.exp2(z[:64]) * (1.0 - s * s) * (jnp.tanh(z[128:]) * 0.5 + 1.0)
    return split(tile)

def first(vt, b, th, tl):
    y = jnp.dot(vt[b], jnp.concatenate([th, tl, th], 0), preferred_element_type=F32)
    return split(y)

def second(dw, b, th, tl, ih, il):
    o = lax.dot_general(jnp.concatenate([th, th, tl], 1), jnp.concatenate([ih, il, ih], 1), (((1,), (1,)), ((), ())), preferred_element_type=F32)
    return jnp.concatenate([o[:32], o[32:]], 1) * (dw[b] * 0.05)

MESH = pl.DeviceIdType.MESH
N = 128
UC = 16


def rows8(g):
    return pl.ds(pl.multiple_of(g * 8, 8), 8)


def local(src, dst, sem):
    return pltpu.make_async_copy(src, dst, sem)


def remote(src, dst, send, recv, where):
    return pltpu.make_async_remote_copy(src, dst, send, recv, device_id=where, device_id_type=MESH)


def gather_kernel(own_h, seg_h, tool_h, vec_h, cols_h, rec_h, act_h, s_h, iw,
                  own_v, seg_v, tool, vec, cols, rec, act, s_v, slot_v, slot,
                  req_s, req_m, req_r, resp, got, lo, hi, sw, vw, nat, bv, vt, at, dw, rw, ft, lhs,
                  ls, gs, ss1, rs1, ss2, rs2, ss3, rs3, hs, hr):
    loads = [local(a, b, ls.at[i]) for i, (a, b) in enumerate(
        ((own_h, own_v), (seg_h, seg_v), (act_h, act), (vec_h, vec), (rec_h, rec), (tool_h, tool), (cols_h, cols)))]
    for c in loads:
        c.start()

    def stiff(g):
        return local(s_h.at[:, rows8(g), :], s_v.at[:, rows8(g), :], gs.at[g])

    for g in range(8):
        stiff(g).start()
    dom, tl = lax.axis_index("dom"), lax.axis_index("tool")
    me = dom * 8 + tl
    px, py = dom // 4, lax.rem(dom, 4)
    span = [(lax.rem(px + a, 4) * 4 + lax.rem(py + b, 4), tl)
            for a, b in ((2, 2), (2, 1), (2, 3), (1, 2), (3, 2), (1, 1), (1, 3), (3, 1), (3, 3), (2, 0), (0, 2), (1, 0), (3, 0), (0, 1), (0, 3))]
    part = [(dom, lax.rem(tl + j, 8)) for j in (4, 3, 5, 2, 6, 1, 7)]
    nxt, prv = lax.rem(me + 1, N), lax.rem(me + N - 1, N)
    after, before = (nxt // 8, lax.rem(nxt, 8)), (prv // 8, lax.rem(prv, 8))
    barrier = pltpu.get_barrier_semaphore()
    for where in span + part + [after, before]:
        pl.semaphore_signal(barrier, inc=1, device_id=where, device_id_type=MESH)
    loads[0].wait()
    loads[1].wait()
    own = jnp.concatenate([own_v[0:1, :], own_v[1:2, :]], axis=1)
    seg = jnp.concatenate([seg_v[0:1, :], seg_v[1:2, :]], axis=1)
    row, col = iota((N, N), 0), iota((N, N), 1)
    hit = jnp.broadcast_to(lax.rem(own, 8) * 16 + own // 8, (N, N)) == row
    key = jnp.broadcast_to(col[0:1] * 256 + seg, (N, N))
    kmin = jnp.min(jnp.where(hit, key, 1 << 20), axis=1, keepdims=True)
    kmax = jnp.max(jnp.where(hit, key, 0), axis=1, keepdims=True)
    req_s[...] = (jnp.where(col == 0, kmin, kmax) & 255).reshape(8, 16, 1, N)
    slot_v[...] = own * 2 + jnp.sum(jnp.where(hit & (key != kmin), 1, 0), axis=0, keepdims=True)
    loads[2].wait()
    prep_act(act, at, dw)
    loads[3].wait()
    vww = vw.at[pl.ds(192, 68 * 32)]

    def relay(g, c):
        to_w(vec[rows8(g), :], vw, 256 + g * 256)
        return c

    lax.fori_loop(0, 8, relay, 0)
    pl.semaphore_wait(barrier, 24)
    local(req_s.at[tl], req_m.at[tl], rs1).start()
    for where in part:
        remote(req_s.at[where[1]], req_m.at[tl], ss1, rs1, where).start()
    down = remote(vec_h.at[pl.ds(56, 8)], lo, hs.at[0], hr.at[0], after)
    up = remote(vec_h.at[pl.ds(0, 8)], hi, hs.at[1], hr.at[1], before)
    down.start()
    up.start()
    keep = local(slot_v, slot, ls.at[7])
    keep.start()

    def pv(g, c):
        for u in range(4):
            prep_vec(vww, nat.at[u], bv, g * 4 + u + 2, g * 4 + u, vt, dw)
        return c

    lax.fori_loop(0, 16, pv, 0)
    local(req_m, req_m, rs1).wait()
    local(req_m.at[:, dom], req_r.at[dom], rs3).start()
    for where in span:
        remote(req_m.at[:, where[0]], req_r.at[dom], ss3, rs3, where).start()
    loads[4].wait()
    for b0 in range(8):
        for f in range(4):
            rw[pl.ds(b0 * 32 + f, 8, stride=4), :] = rec[b0 * 8:b0 * 8 + 8, f * 128:(f + 1) * 128]

    def pp(g, c):
        for u in range(2):
            prep_part(rw, ft, lhs, g * 2 + u, u)
        return c

    lax.fori_loop(0, 16, pp, 0)
    loads[5].wait()
    local(req_r, req_r, rs3).wait()
    ask = req_r[...].reshape(N, N)
    for r in range(2):
        hot = (iota((N, 256), 1) == ask[:, r:r + 1]).astype(F32)
        g = jnp.dot(hot, tool[...], precision=lax.Precision.HIGHEST, preferred_element_type=F32)
        for f in range(4):
            resp[:, r * 4 + f, :] = g[:, f * 128:(f + 1) * 128]
    local(resp.at[me], got.at[me], rs2).start()

    def reply(j, c):
        d = lax.rem(me + j, N)
        remote(resp.at[d], got.at[me], ss2, rs2, (d // 8, lax.rem(d, 8))).start()
        return c

    lax.fori_loop(1, N, reply, 0, unroll=2)
    down.wait()
    up.wait()

    @pl.when(me == 0)
    def _():
        lo[...] = jnp.zeros_like(lo)

    @pl.when(me == N - 1)
    def _():
        hi[...] = jnp.zeros_like(hi)

    to_w(lo, vw, 0)
    to_w(hi, vw, 256 + 2048)
    for i, c in enumerate((0, 1, 66, 67)):
        prep_vec(vww, nat.at[i], bv, c, None, vt, dw)
    loads[6].wait()

    def ig(g, c):
        stiff(g).wait()
        for e in range(E5):
            to_w(s_v[e, rows8(g), :], sw.at[e], 0)
        for bb in range(8):
            inner_block(cols, sw, bv, iw, g * 8 + bb, bb)
        return c

    lax.fori_loop(0, 8, ig, 0)
    keep.wait()
    local(req_s.at[pl.ds(0, 7)], req_s.at[pl.ds(0, 7)], ss1).wait()
    local(req_r.at[pl.ds(0, 15)], req_r.at[pl.ds(0, 15)], ss3).wait()
    local(got, got, rs2).wait()

    def cg(g, c):
        bs = [g * UC + u for u in range(UC)]
        t = [tile_of(slot, got, lhs, b) for b in bs]
        y = [first(vt, b, *x) for b, x in zip(bs, t)]
        z = [second(dw, b, *x, *w) for b, x, w in zip(bs, t, y)]
        at32 = [pl.ds(pl.multiple_of(b * 32, 32), 32) for b in bs]
        total = [iw[a, :] + w for a, w in zip(at32, z)]
        for a, w in zip(at32, total):
            iw[a, :] = w
        return c

    lax.fori_loop(0, NB // UC, cg, 0)
    local(resp.at[pl.ds(0, N - 1)], resp.at[pl.ds(0, N - 1)], ss2).wait()


def layout_kernel(iw, out_h, out, os):
    def save(g):
        return local(out.at[rows8(g), :], out_h.at[rows8(g), :], os.at[g])

    def og(g, c):
        for t in range(32):
            out[rows8(g), t * 128:(t + 1) * 128] = iw[pl.ds(g * 256 + t, 8, stride=32), :]
        save(g).start()
        return c

    lax.fori_loop(0, 8, og, 0)
    for g in range(8):
        save(g).wait()


def per_device(records, tool_data, owners, local_seg, active, stiffness, columns, vectors):
    vm, sm, dma = pltpu.VMEM, pltpu.SMEM, pltpu.SemaphoreType.DMA
    i32 = jnp.int32
    whole = pl.BlockSpec(memory_space=vm)
    far = pl.BlockSpec(memory_space=pl.ANY)
    iw = pl.pallas_call(
        gather_kernel,
        out_shape=jax.ShapeDtypeStruct((NB * 32, 128), F32),
        in_specs=[far] * 8,
        out_specs=whole,
        scratch_shapes=[
            vm((2, NB), i32), vm((2, NB), i32), vm((256, 512), F32), vm((NB, 4096), F32), sm((E5, NB), i32),
            vm((NB, 512), F32), vm((NB, 64), i32), vm((E5, NB, 4096), F32), vm((1, N), i32), sm((1, N), i32),
            vm((8, 16, 1, N), i32), vm((8, 16, 1, N), i32), vm((16, 8, 1, N), i32), vm((N, 8, 128), F32), vm((N, 8, 128), F32),
            vm((8, 4096), F32), vm((8, 4096), F32),
            vm((E5, 256, 128), F32), vm((80 * 32, 128), F32), vm((4, 64, 128), F32), vm((68, 128, 256), BF16),
            vm((NB, 64, 192), BF16), vm((64, 64), F32), vm((NB, 32, 128), F32), vm((256, 128), F32),
            vm((3, 2, 128, 64), F32), vm((NB, 192, 64), BF16),
            dma((8,)), dma((8,)), dma, dma, dma, dma, dma, dma, dma((2,)), dma((2,)),
        ],
        compiler_params=pltpu.CompilerParams(collective_id=0, has_side_effects=True, vmem_limit_bytes=60 << 20),
        name="gather_rows",
    )(owners.T, local_seg.T, tool_data, vectors, columns.T, records, active, stiffness.transpose(1, 0, 2))
    return pl.pallas_call(
        layout_kernel,
        out_shape=jax.ShapeDtypeStruct((NB, 4096), F32),
        in_specs=[whole],
        out_specs=far,
        scratch_shapes=[vm((NB, 4096), F32), dma((8,))],
        compiler_params=pltpu.CompilerParams(vmem_limit_bytes=16 << 20),
        name="layout",
    )(iw)


def solution(mesh):
    ax = P(("dom", "tool"), None)
    return jax.shard_map(per_device, mesh=mesh, in_specs=(ax,) * 5 + (P(("dom", "tool"), None, None), ax, ax), out_specs=ax, check_vma=False)
```

```python
import math
import jax
import jax.numpy as jnp
import numpy as np
from jax import lax
from jax.experimental import pallas as pl
from jax.experimental.pallas import tpu as pltpu
from jax.sharding import PartitionSpec as P
F32, BF16 = jnp.float32, jnp.bfloat16
NB, HB, E5 = 64, 2, 5
A2 = math.log2(math.e) / 8.0
TURN = 1.0 / (2.0 * math.pi)
def fit():
    r = np.cos(np.linspace(0, np.pi / 2, 4001))[:-1] * 0.5
    w = np.sqrt(2.0) * np.sin(np.pi * r) / r
    a = np.stack([r ** (2 * k) for k in range(5)], 1)
    c = np.linalg.lstsq(a * r[:, None], w * r, rcond=None)[0]
    return [float(x) for x in c]


SINC = fit()

def iota(shape, dim):
    return lax.broadcasted_iota(jnp.int32, shape, dim)

def split(x):
    hi = x.astype(BF16)
    return hi, (x - hi.astype(F32)).astype(BF16)

def split3(x):
    h = x.astype(BF16).astype(F32)
    y = x - h
    m = y.astype(BF16).astype(F32)
    return h, m, y - m

def pair8(g0, g1):
    lane = iota((4, 128), 1)
    ev = jnp.where(lane < 64, g0, pltpu.roll(g1, 64, 1))
    od = jnp.where(lane < 64, pltpu.roll(g0, 64, 1), g1)
    return jnp.concatenate([ev, od], 0)

def mask_rows(which):
    s = iota((8, 128), 0)
    m = s == which[0]
    for w in which[1:]:
        m = m | (s == w)
    return m

def square_sum(x):
    return jnp.sum(jnp.where(mask_rows((0, 1, 4)), x * x, 0.0), 0, keepdims=True) * A2

def prep_vec(w, nat, bv, c, own_b, vt, dw):
    lane = iota((32, 128), 1)
    wr = pltpu.roll(w, 64, 1)
    nat[pl.ds(0, 32, stride=2), :] = jnp.where(lane < 64, w, wr)
    nat[pl.ds(1, 32, stride=2), :] = jnp.where(lane < 64, wr, w)
    d = nat[...]
    lane2 = iota((64, 128), 1)
    h, l = split(d)
    z = jnp.zeros_like(h)
    lo, up = lane2 < 64, lane2 >= 64
    bv[c] = jnp.concatenate([jnp.concatenate([jnp.where(lo, h, z), jnp.where(lo, l, z)], 1),
                             jnp.concatenate([jnp.where(up, h, z), jnp.where(up, l, z)], 1)], 0)
    if own_b is not None:
        w = w * dw[own_b]
        t = jnp.concatenate([w[:, :64], w[:, 64:]], 0).T
        h, l = split(t)
        vt[own_b] = jnp.concatenate([h, h, l], 1)

def prep_act(act, at, dw):
    at[...] = act[...].astype(F32).T
    a = jnp.concatenate([at[pl.ds(0, 32, stride=2), :], at[pl.ds(1, 32, stride=2), :]], 1).astype(BF16)
    row, col = iota((128, 128), 0), iota((128, 128), 1)
    same = (row // 64) == (col // 64)
    def one(g, carry):
        for k in range(16):
            b = g * 16 + k
            hot = jnp.where(same & (lax.rem(row, 64) == b), 1.0, 0.0).astype(BF16)
            dw[b] = jnp.dot(a, hot, preferred_element_type=F32)
        return carry
    lax.fori_loop(0, 4, one, 0)

def prep_part(rw, ft, lhs, g, k):
    p = pair8(rw[g // 4, lax.rem(g, 4) * 2], rw[g // 4, lax.rem(g, 4) * 2 + 1])
    sub = iota((8, 128), 0)
    pos = mask_rows((0, 1, 4))
    ph, pm, pl_ = split3(-square_sum(p))
    extra = jnp.where(sub < 3, -1.0, jnp.where(sub == 3, ph, jnp.where(sub == 4, pm, jnp.where(sub == 5, pl_, 0.0))))
    scale = jnp.where(pos, 2.0 * A2, jnp.where(sub == 7, 1.0, jnp.where(sub == 3, TURN, 3.0 * TURN)))
    h, m, l = split3(p * scale)
    zero = jnp.zeros_like(h)
    for n, mk in enumerate((pos, mask_rows((2, 3, 5, 6)), sub == 7)):
        hh, mm, ll = (jnp.where(mk, x, 0.0) for x in (h, m, l))
        f = jnp.concatenate([hh, hh, hh, mm, mm, ll, extra if n == 0 else zero, zero], 0)
        ft[n, k] = f.T
    for q in range(2):
        parts = []
        for n in range(3):
            for par in range(2):
                parts.append(ft[n, k, pl.ds(q * 64 + par, 32, stride=2), :])
        lhs[g * 2 + q] = jnp.concatenate(parts, 0).astype(BF16)

def inner_block(cols, sw, bv, b, bb):
    w = jnp.concatenate([sw[e, b // 8, bb] for e in range(E5)], 1)
    h, l = split(w)
    r = jnp.concatenate([bv[cols[e, b]] for e in range(E5)], 0)
    o = jnp.dot(jnp.concatenate([h, l], 0), r, preferred_element_type=F32)
    return (o[:32, :128] + o[:32, 128:]) + (o[32:, :128] + o[32:, 128:])


def cand_rows(got, s):
    x = got[s // 2]
    return jnp.where(lax.rem(s, 2) == 1, x[4:8], x[0:4])

def tile_of(slot, got, lhs, b):
    x = pair8(cand_rows(got, slot[0, b]), cand_rows(got, slot[0, NB + b]))
    sub = iota((8, 128), 0)
    h, m, l = split3(x)
    qh, qm, ql = split3(square_sum(x))
    extra = jnp.where(sub == 0, qh, jnp.where(sub == 1, qm, jnp.where(sub == 2, ql, jnp.where(sub < 6, 1.0, 0.0))))
    rhs = jnp.concatenate([h, m, l, h, m, h, extra, jnp.zeros_like(h)], 0).astype(BF16)
    z = jnp.dot(lhs[b], rhs, preferred_element_type=F32)
    x = z[64:128]
    r = x - jnp.round(x)
    r2 = r * r
    s = SINC[4]
    for c in SINC[3::-1]:
        s = s * r2 + c
    s = s * r
    tile = jnp.exp2(z[:64]) * (1.0 - s * s) * (jnp.tanh(z[128:]) * 0.5 + 1.0)
    return split(tile)

def first(vt, b, th, tl):
    y = jnp.dot(vt[b], jnp.concatenate([th, tl, th], 0), preferred_element_type=F32)
    return split(y)

def second(dw, b, th, tl, ih, il):
    o = lax.dot_general(jnp.concatenate([th, th, tl], 1), jnp.concatenate([ih, il, ih], 1), (((1,), (1,)), ((), ())), preferred_element_type=F32)
    return jnp.concatenate([o[:32], o[32:]], 1) * (dw[b] * 0.05)

MESH = pl.DeviceIdType.MESH
N = 128
UC = 16


def rows8(g):
    return pl.ds(pl.multiple_of(g * 8, 8), 8)


def local(src, dst, sem):
    return pltpu.make_async_copy(src, dst, sem)


def remote(src, dst, send, recv, where):
    return pltpu.make_async_remote_copy(src, dst, send, recv, device_id=where, device_id_type=MESH)


def gather_kernel(own_h, seg_h, tool_h, vec_h, cols_h, rec_h, act_h, s_h, iw_h,
                  own_v, seg_v, tool, vw, cols, rw, act, sw, slot_v, slot,
                  req_s, req_m, req_r, resp, got, lo, hi, iw, nat, bv, vt, at, dw, ft, lhs,
                  ls, ws, vs, fs, gs, ss1, rs1, ss2, rs2, ss3, rs3, hs, hr):
    loads = [local(a, b, ls.at[i]) for i, (a, b) in enumerate(
        ((own_h, own_v), (seg_h, seg_v), (act_h, act), (tool_h, tool), (cols_h, cols)))]
    for c in loads[:3]:
        c.start()
    for k in range(8):
        local(vec_h.at[:, :, k], vw.at[:, k], vs).start()
    for k in range(8):
        local(rec_h.at[:, :, k], rw.at[:, k], fs).start()
    for c in loads[3:]:
        c.start()
    dom, tl = lax.axis_index("dom"), lax.axis_index("tool")
    me = dom * 8 + tl
    px, py = dom // 4, lax.rem(dom, 4)
    span = [(lax.rem(px + a, 4) * 4 + lax.rem(py + b, 4), tl)
            for a, b in ((2, 2), (2, 1), (2, 3), (1, 2), (3, 2), (1, 1), (1, 3), (3, 1), (3, 3), (2, 0), (0, 2), (1, 0), (3, 0), (0, 1), (0, 3))]
    part = [(dom, lax.rem(tl + j, 8)) for j in (4, 3, 5, 2, 6, 1, 7)]
    nxt, prv = lax.rem(me + 1, N), lax.rem(me + N - 1, N)
    after, before = (nxt // 8, lax.rem(nxt, 8)), (prv // 8, lax.rem(prv, 8))
    barrier = pltpu.get_barrier_semaphore()
    for where in span + part + [after, before]:
        pl.semaphore_signal(barrier, inc=1, device_id=where, device_id_type=MESH)
    for k in range(8):
        local(s_h.at[:, :, :, k], sw.at[:, :, k], gs).start()
    loads[0].wait()
    loads[1].wait()
    own = jnp.concatenate([own_v[0:1, :], own_v[1:2, :]], axis=1)
    seg = jnp.concatenate([seg_v[0:1, :], seg_v[1:2, :]], axis=1)
    row, col = iota((N, N), 0), iota((N, N), 1)
    hit = jnp.broadcast_to(lax.rem(own, 8) * 16 + own // 8, (N, N)) == row
    key = jnp.broadcast_to(col[0:1] * 256 + seg, (N, N))
    kmin = jnp.min(jnp.where(hit, key, 1 << 20), axis=1, keepdims=True)
    kmax = jnp.max(jnp.where(hit, key, 0), axis=1, keepdims=True)
    req_s[...] = (jnp.where(col == 0, kmin, kmax) & 255).reshape(8, 16, 1, N)
    slot_v[...] = own * 2 + jnp.sum(jnp.where(hit & (key != kmin), 1, 0), axis=0, keepdims=True)
    loads[2].wait()
    prep_act(act, at, dw)
    pl.semaphore_wait(barrier, 24)
    local(req_s.at[tl], req_m.at[tl], rs1).start()
    for where in part:
        remote(req_s.at[where[1]], req_m.at[tl], ss1, rs1, where).start()
    halo = [remote(vec_h.at[7, :, 6 + k], lo.at[k], hs.at[k], hr.at[k], after) for k in range(HB)]
    halo += [remote(vec_h.at[0, :, k], hi.at[k], hs.at[HB + k], hr.at[HB + k], before) for k in range(HB)]
    for c in halo:
        c.start()
    keep = local(slot_v, slot, ls.at[7])
    keep.start()

    local(vw, vw, vs).wait()

    def pv(g, c):
        for u in range(4):
            b = g * 4 + u
            prep_vec(vw[g // 2, lax.rem(g, 2) * 4 + u], nat.at[u], bv, b + HB, b, vt, dw)
        return c

    lax.fori_loop(0, 16, pv, 0)
    local(req_m, req_m, rs1).wait()
    local(req_m.at[:, dom], req_r.at[dom], rs3).start()
    for where in span:
        remote(req_m.at[:, where[0]], req_r.at[dom], ss3, rs3, where).start()
    local(rw, rw, fs).wait()

    def pp(g, c):
        for u in range(4):
            prep_part(rw, ft, lhs, g * 4 + u, u)
        return c

    lax.fori_loop(0, 8, pp, 0)
    loads[3].wait()
    local(req_r, req_r, rs3).wait()
    ask = req_r[...].reshape(N, N)
    for r in range(2):
        hot = (iota((N, 256), 1) == ask[:, r:r + 1]).astype(F32)
        g = jnp.dot(hot, tool[...], precision=lax.Precision.HIGHEST, preferred_element_type=F32)
        for f in range(4):
            resp[:, r * 4 + f, :] = g[:, f * 128:(f + 1) * 128]
    local(resp.at[me], got.at[me], rs2).start()

    def reply(j, c):
        d = lax.rem(me + j, N)
        remote(resp.at[d], got.at[me], ss2, rs2, (d // 8, lax.rem(d, 8))).start()
        return c

    lax.fori_loop(1, N, reply, 0, unroll=2)
    for c in halo:
        c.wait()

    @pl.when(me == 0)
    def _():
        lo[...] = jnp.zeros_like(lo)

    @pl.when(me == N - 1)
    def _():
        hi[...] = jnp.zeros_like(hi)

    for k in range(HB):
        prep_vec(lo[k], nat.at[k], bv, k, None, vt, dw)
        prep_vec(hi[k], nat.at[HB + k], bv, HB + NB + k, None, vt, dw)
    loads[4].wait()
    local(sw, sw, gs).wait()

    def ig(g, c):
        z = [inner_block(cols, sw, bv, g * 8 + u, u) for u in range(8)]
        for u in range(8):
            iw[g, u] = z[u]
        return c

    lax.fori_loop(0, 8, ig, 0)
    keep.wait()
    local(req_s.at[pl.ds(0, 7)], req_s.at[pl.ds(0, 7)], ss1).wait()
    local(req_r.at[pl.ds(0, 15)], req_r.at[pl.ds(0, 15)], ss3).wait()
    local(got, got, rs2).wait()

    def leave(g):
        block = pl.ds(g * (UC // 8), UC // 8)
        return local(iw.at[block], iw_h.at[block], ws.at[g])

    def cg(g, c):
        bs = [g * UC + u for u in range(UC)]
        t = [tile_of(slot, got, lhs, b) for b in bs]
        y = [first(vt, b, *x) for b, x in zip(bs, t)]
        z = [second(dw, b, *x, *w) for b, x, w in zip(bs, t, y)]
        spot = [(g * (UC // 8) + u // 8, u % 8) for u in range(UC)]
        total = [iw[p] + w for p, w in zip(spot, z)]
        for p, w in zip(spot, total):
            iw[p] = w
        leave(g).start()
        return c

    lax.fori_loop(0, NB // UC, cg, 0)
    for g in range(NB // UC):
        leave(g).wait()
    local(resp.at[pl.ds(0, N - 1)], resp.at[pl.ds(0, N - 1)], ss2).wait()


def layout_kernel(iw_h, out_h, iw, ws, os):
    def load(k):
        return local(iw_h.at[:, k], iw.at[:, k], ws.at[k])

    def save(k):
        return local(iw.at[:, k], out_h.at[:, :, k], os.at[k])

    for k in range(8):
        load(k).start()
    for k in range(8):
        load(k).wait()
        save(k).start()
    for k in range(8):
        save(k).wait()


def sublanes_last(x):
    return x.reshape(8, 8, -1, 128).transpose(0, 2, 1, 3)


def per_device(records, tool_data, owners, local_seg, active, stiffness, columns, vectors):
    vm, sm, dma = pltpu.VMEM, pltpu.SMEM, pltpu.SemaphoreType.DMA
    i32 = jnp.int32
    far = pl.BlockSpec(memory_space=pl.ANY)
    iw = pl.pallas_call(
        gather_kernel,
        out_shape=jax.ShapeDtypeStruct((8, 8, 32, 128), F32),
        in_specs=[far] * 8,
        out_specs=far,
        scratch_shapes=[
            vm((2, NB), i32), vm((2, NB), i32), vm((256, 512), F32), vm((8, 8, 32, 128), F32), sm((E5, NB), i32),
            vm((8, 8, 4, 128), F32), vm((NB, 64), i32), vm((E5, 8, 8, 32, 128), F32), vm((1, N), i32), sm((1, N), i32),
            vm((8, 16, 1, N), i32), vm((8, 16, 1, N), i32), vm((16, 8, 1, N), i32), vm((N, 8, 128), F32), vm((N, 8, 128), F32),
            vm((HB, 32, 128), F32), vm((HB, 32, 128), F32), vm((8, 8, 32, 128), F32),
            vm((4, 64, 128), F32), vm((68, 128, 256), BF16), vm((NB, 64, 192), BF16), vm((64, 64), F32),
            vm((NB, 32, 128), F32), vm((3, 4, 128, 64), F32), vm((NB, 192, 64), BF16),
            dma((8,)), dma((NB // UC,)), dma, dma, dma, dma, dma, dma, dma, dma, dma, dma((2 * HB,)), dma((2 * HB,)),
        ],
        compiler_params=pltpu.CompilerParams(collective_id=0, has_side_effects=True, vmem_limit_bytes=60 << 20),
        name="gather_rows",
    )(owners.T, local_seg.T, tool_data, sublanes_last(vectors), columns.T, sublanes_last(records), active,
      stiffness.transpose(1, 0, 2).reshape(E5, 8, 8, 32, 128).transpose(0, 1, 3, 2, 4))
    out = pl.pallas_call(
        layout_kernel,
        out_shape=jax.ShapeDtypeStruct((8, 32, 8, 128), F32),
        in_specs=[far],
        out_specs=far,
        scratch_shapes=[vm((8, 8, 32, 128), F32), dma((8,)), dma((8,))],
        compiler_params=pltpu.CompilerParams(vmem_limit_bytes=60 << 20),
        name="layout",
    )(iw)
    return out.transpose(0, 2, 1, 3).reshape(NB, 4096)


def solution(mesh):
    ax = P(("dom", "tool"), None)
    return jax.shard_map(per_device, mesh=mesh, in_specs=(ax,) * 5 + (P(("dom", "tool"), None, None), ax, ax), out_specs=ax, check_vma=False)
```

```python
import math
import jax
import jax.numpy as jnp
import numpy as np
from jax import lax
from jax.experimental import pallas as pl
from jax.experimental.pallas import tpu as pltpu
from jax.sharding import PartitionSpec as P
F32, BF16 = jnp.float32, jnp.bfloat16
NB, HB, E5 = 64, 2, 5
A2 = math.log2(math.e) / 8.0
TURN = 1.0 / (2.0 * math.pi)
def fit():
    r = np.cos(np.linspace(0, np.pi / 2, 4001))[:-1] * 0.5
    w = np.sqrt(2.0) * np.sin(np.pi * r) / r
    a = np.stack([r ** (2 * k) for k in range(5)], 1)
    c = np.linalg.lstsq(a * r[:, None], w * r, rcond=None)[0]
    return [float(x) for x in c]


SINC = fit()

def iota(shape, dim):
    return lax.broadcasted_iota(jnp.int32, shape, dim)

def split(x):
    hi = x.astype(BF16)
    return hi, (x - hi.astype(F32)).astype(BF16)

def split3(x):
    h = x.astype(BF16).astype(F32)
    y = x - h
    m = y.astype(BF16).astype(F32)
    return h, m, y - m

def pair8(g0, g1):
    lane = iota((4, 128), 1)
    ev = jnp.where(lane < 64, g0, pltpu.roll(g1, 64, 1))
    od = jnp.where(lane < 64, pltpu.roll(g0, 64, 1), g1)
    return jnp.concatenate([ev, od], 0)

def mask_rows(which):
    s = iota((8, 128), 0)
    m = s == which[0]
    for w in which[1:]:
        m = m | (s == w)
    return m

def square_sum(x):
    return jnp.sum(jnp.where(mask_rows((0, 1, 4)), x * x, 0.0), 0, keepdims=True) * A2

def prep_vec(w, nat, bv, c, own_b, vt, dw):
    lane = iota((32, 128), 1)
    wr = pltpu.roll(w, 64, 1)
    nat[pl.ds(0, 32, stride=2), :] = jnp.where(lane < 64, w, wr)
    nat[pl.ds(1, 32, stride=2), :] = jnp.where(lane < 64, wr, w)
    d = nat[...]
    lane2 = iota((64, 128), 1)
    h, l = split(d)
    z = jnp.zeros_like(h)
    lo, up = lane2 < 64, lane2 >= 64
    bv[c] = jnp.concatenate([jnp.concatenate([jnp.where(lo, h, z), jnp.where(lo, l, z)], 1),
                             jnp.concatenate([jnp.where(up, h, z), jnp.where(up, l, z)], 1)], 0)
    if own_b is not None:
        w = w * dw[own_b]
        t = jnp.concatenate([w[:, :64], w[:, 64:]], 0).T
        h, l = split(t)
        vt[own_b] = jnp.concatenate([h, h, l], 1)

def prep_act(act, at, dw):
    at[...] = act[...].astype(F32).T
    a = jnp.concatenate([at[pl.ds(0, 32, stride=2), :], at[pl.ds(1, 32, stride=2), :]], 1).astype(BF16)
    row, col = iota((128, 128), 0), iota((128, 128), 1)
    same = (row // 64) == (col // 64)
    def one(g, carry):
        for k in range(16):
            b = g * 16 + k
            hot = jnp.where(same & (lax.rem(row, 64) == b), 1.0, 0.0).astype(BF16)
            dw[b] = jnp.dot(a, hot, preferred_element_type=F32)
        return carry
    lax.fori_loop(0, 4, one, 0)

def prep_part(rw, ft, lhs, g, k):
    p = pair8(rw[g // 4, lax.rem(g, 4) * 2], rw[g // 4, lax.rem(g, 4) * 2 + 1])
    sub = iota((8, 128), 0)
    pos = mask_rows((0, 1, 4))
    ph, pm, pl_ = split3(-square_sum(p))
    extra = jnp.where(sub < 3, -1.0, jnp.where(sub == 3, ph, jnp.where(sub == 4, pm, jnp.where(sub == 5, pl_, 0.0))))
    scale = jnp.where(pos, 2.0 * A2, jnp.where(sub == 7, 1.0, jnp.where(sub == 3, TURN, 3.0 * TURN)))
    h, m, l = split3(p * scale)
    zero = jnp.zeros_like(h)
    for n, mk in enumerate((pos, mask_rows((2, 3, 5, 6)), sub == 7)):
        hh, mm, ll = (jnp.where(mk, x, 0.0) for x in (h, m, l))
        f = jnp.concatenate([hh, hh, hh, mm, mm, ll, extra if n == 0 else zero, zero], 0)
        ft[n, k] = f.T
    for q in range(2):
        parts = []
        for n in range(3):
            for par in range(2):
                parts.append(ft[n, k, pl.ds(q * 64 + par, 32, stride=2), :])
        lhs[g * 2 + q] = jnp.concatenate(parts, 0).astype(BF16)

def inner_block(cols, sw, bv, b, bb):
    w = jnp.concatenate([sw[e, b // 8, bb] for e in range(E5)], 1)
    h, l = split(w)
    r = jnp.concatenate([bv[cols[e, b]] for e in range(E5)], 0)
    o = jnp.dot(jnp.concatenate([h, l], 0), r, preferred_element_type=F32)
    return (o[:32, :128] + o[:32, 128:]) + (o[32:, :128] + o[32:, 128:])


def cand_rows(got, s):
    x = got[s // 2]
    return jnp.where(lax.rem(s, 2) == 1, x[4:8], x[0:4])

def tile_of(xt, lhs, b):
    x = xt[b]
    sub = iota((8, 128), 0)
    h, m, l = split3(x)
    qh, qm, ql = split3(square_sum(x))
    extra = jnp.where(sub == 0, qh, jnp.where(sub == 1, qm, jnp.where(sub == 2, ql, jnp.where(sub < 6, 1.0, 0.0))))
    rhs = jnp.concatenate([h, m, l, h, m, h, extra, jnp.zeros_like(h)], 0).astype(BF16)
    z = jnp.dot(lhs[b], rhs, preferred_element_type=F32)
    x = z[64:128]
    r = x - jnp.round(x)
    r2 = r * r
    s = SINC[4]
    for c in SINC[3::-1]:
        s = s * r2 + c
    s = s * r
    tile = jnp.exp2(z[:64]) * (1.0 - s * s) * (jnp.tanh(z[128:]) * 0.5 + 1.0)
    return split(tile)

def first(vt, b, th, tl):
    y = jnp.dot(vt[b], jnp.concatenate([th, tl, th], 0), preferred_element_type=F32)
    return split(y)

def second(dw, b, th, tl, ih, il):
    o = lax.dot_general(jnp.concatenate([th, th, tl], 1), jnp.concatenate([ih, il, ih], 1), (((1,), (1,)), ((), ())), preferred_element_type=F32)
    return jnp.concatenate([o[:32], o[32:]], 1) * (dw[b] * 0.05)

MESH = pl.DeviceIdType.MESH
N = 128
UC = 32
PV = 12
RINGS = (((1, 0), (3, 0), (0, 1), (0, 3), (0, 0)), ((2, 0), (0, 2), (1, 1), (1, 3), (3, 1), (3, 3)), ((2, 1), (2, 3), (1, 2), (3, 2)), ((2, 2),))


def rows8(g):
    return pl.ds(pl.multiple_of(g * 8, 8), 8)


def local(src, dst, sem):
    return pltpu.make_async_copy(src, dst, sem)


def remote(src, dst, send, recv, where):
    return pltpu.make_async_remote_copy(src, dst, send, recv, device_id=where, device_id_type=MESH)


def gather_kernel(own_h, seg_h, tool_h, vec_h, cols_h, rec_h, act_h, s_h, xt, lhs, vt, dw, iw,
                  own_v, seg_v, tool, vw, cols, rw, act, sw, slot_v, slot,
                  req_s, req_m, req_r, resp, got, lo, hi, nat, bv, at, ft, tool3,
                  ls, vs, fs, gs, ss1, rs1, ss2, rs2, ss3, rs3, hs, hr):
    loads = [local(a, b, ls.at[i]) for i, (a, b) in enumerate(
        ((own_h, own_v), (seg_h, seg_v), (act_h, act), (tool_h, tool), (cols_h, cols)))]
    for c in loads[:2]:
        c.start()
    dom, tl = lax.axis_index("dom"), lax.axis_index("tool")
    me = dom * 8 + tl
    px, py = dom // 4, lax.rem(dom, 4)
    span = [(lax.rem(px + a, 4) * 4 + lax.rem(py + b, 4), tl)
            for a, b in ((2, 2), (2, 1), (2, 3), (1, 2), (3, 2), (1, 1), (1, 3), (3, 1), (3, 3), (2, 0), (0, 2), (1, 0), (3, 0), (0, 1), (0, 3))]
    part = [(dom, lax.rem(tl + j, 8)) for j in (4, 3, 5, 2, 6, 1, 7)]
    nxt, prv = lax.rem(me + 1, N), lax.rem(me + N - 1, N)
    after, before = (nxt // 8, lax.rem(nxt, 8)), (prv // 8, lax.rem(prv, 8))
    barrier = pltpu.get_barrier_semaphore()
    for where in span + part + [after, before]:
        pl.semaphore_signal(barrier, inc=1, device_id=where, device_id_type=MESH)
    for c in loads[2:]:
        c.start()
    for k in range(8):
        local(vec_h.at[:, :, k], vw.at[:, k], vs).start()
    for k in range(8):
        local(rec_h.at[:, :, k], rw.at[:, k], fs).start()
    for k in range(8):
        local(s_h.at[:, :, :, k], sw.at[:, :, k], gs).start()
    loads[0].wait()
    loads[1].wait()
    own = jnp.concatenate([own_v[0:1, :], own_v[1:2, :]], axis=1)
    seg = jnp.concatenate([seg_v[0:1, :], seg_v[1:2, :]], axis=1)
    row, col = iota((N, N), 0), iota((N, N), 1)
    hit = jnp.broadcast_to(lax.rem(own, 8) * 16 + own // 8, (N, N)) == row
    key = jnp.broadcast_to(col[0:1] * 256 + seg, (N, N))
    kmin = jnp.min(jnp.where(hit, key, 1 << 20), axis=1, keepdims=True)
    kmax = jnp.max(jnp.where(hit, key, 0), axis=1, keepdims=True)
    req_s[...] = (jnp.where(col == 0, kmin, kmax) & 255).reshape(8, 16, 1, N)
    loads[3].wait()
    for k in range(4):
        for n, x in enumerate(split3(tool[k * 64:(k + 1) * 64, :])):
            tool3[k * 64:(k + 1) * 64, n * 512:(n + 1) * 512] = x.astype(BF16)
    loads[2].wait()
    prep_act(act, at, dw)
    pl.semaphore_wait(barrier, 24)
    local(req_s.at[tl], req_m.at[tl], rs1).start()
    for where in part:
        remote(req_s.at[where[1]], req_m.at[tl], ss1, rs1, where).start()
    halo = [remote(vec_h.at[7, :, 6 + k], lo.at[k], hs.at[k], hr.at[k], after) for k in range(HB)]
    halo += [remote(vec_h.at[0, :, k], hi.at[k], hs.at[HB + k], hr.at[HB + k], before) for k in range(HB)]
    for c in halo:
        c.start()
    slot_v[...] = own * 2 + jnp.sum(jnp.where(hit & (key != kmin), 1, 0), axis=0, keepdims=True)

    local(vw, vw, vs).wait()

    def pv(g, c):
        for u in range(4):
            b = g * 4 + u
            prep_vec(vw[g // 2, lax.rem(g, 2) * 4 + u], nat.at[u], bv, b + HB, b, vt, dw)
        return c

    lax.fori_loop(0, PV, pv, 0)
    local(req_m, req_m, rs1).wait()
    local(req_m.at[:, dom], req_r.at[dom], rs3.at[dom]).start()
    for where in span:
        remote(req_m.at[:, where[0]], req_r.at[dom], ss3, rs3.at[dom], where).start()
    keep = local(slot_v, slot, ls.at[7])
    keep.start()
    lax.fori_loop(PV, 16, pv, 0)
    for ring in RINGS:
        rows = [lax.rem(px + a, 4) * 4 + lax.rem(py + b, 4) for a, b in ring]
        for d in rows:
            local(req_r.at[d], req_r.at[d], rs3.at[d]).wait()
        n = len(rows) * 8
        ask = jnp.concatenate([req_r[d].reshape(8, N) for d in rows], 0)
        hot = jnp.concatenate([(iota((n, 256), 1) == ask[:, r:r + 1]).astype(F32) for r in range(2)], 0).astype(BF16)
        g = jnp.dot(hot, tool3[...], preferred_element_type=F32)
        g = (g[:, :512] + g[:, 512:1024]) + g[:, 1024:]
        for i, d in enumerate(rows):
            for r in range(2):
                for f in range(4):
                    resp[rows8(d), r * 4 + f, :] = g[r * n + i * 8:r * n + i * 8 + 8, f * 128:(f + 1) * 128]
        far = [d for d, at in zip(rows, ring) if at != (0, 0)]
        near = len(far) < len(rows)
        if near:
            local(resp.at[me], got.at[me], rs2).start()

        def reply(j, c, far=far, near=near):
            t = lax.rem(tl + j, 8)
            for d in far:
                remote(resp.at[d * 8 + t], got.at[me], ss2, rs2, (d, t)).start()
            return c

        def beside(j, c):
            t = lax.rem(tl + j, 8)
            remote(resp.at[dom * 8 + t], got.at[me], ss2, rs2, (dom, t)).start()
            return c

        lax.fori_loop(0, 8, reply, 0)
        if near:
            lax.fori_loop(1, 8, beside, 0)
    local(rw, rw, fs).wait()

    def pp(g, c):
        for u in range(4):
            prep_part(rw, ft, lhs, g * 4 + u, u)
        return c

    lax.fori_loop(0, 8, pp, 0)
    for c in halo:
        c.wait()

    @pl.when(me == 0)
    def _():
        lo[...] = jnp.zeros_like(lo)

    @pl.when(me == N - 1)
    def _():
        hi[...] = jnp.zeros_like(hi)

    for k in range(HB):
        prep_vec(lo[k], nat.at[k], bv, k, None, vt, dw)
        prep_vec(hi[k], nat.at[HB + k], bv, HB + NB + k, None, vt, dw)
    loads[4].wait()
    local(sw, sw, gs).wait()

    def ig(g, c):
        z = [inner_block(cols, sw, bv, g * 8 + u, u) for u in range(8)]
        for u in range(8):
            iw[g, u] = z[u]
        return c

    lax.fori_loop(0, 8, ig, 0)
    keep.wait()
    local(req_s.at[pl.ds(0, 7)], req_s.at[pl.ds(0, 7)], ss1).wait()
    local(req_r.at[pl.ds(0, 15)], req_r.at[pl.ds(0, 15)], ss3).wait()
    local(got, got, rs2).wait()

    def pick(g, c):
        for u in range(8):
            b = g * 8 + u
            xt[b] = pair8(cand_rows(got, slot[0, b]), cand_rows(got, slot[0, NB + b]))
        return c

    lax.fori_loop(0, 8, pick, 0)
    local(resp.at[pl.ds(0, N - 1)], resp.at[pl.ds(0, N - 1)], ss2).wait()


def contact_kernel(xt, lhs, vt, dw, iw, out_h, total, os):
    def save(g, k):
        return local(total.at[pl.ds(g * (UC // 8), UC // 8), k], out_h.at[pl.ds(g * (UC // 8), UC // 8), :, k], os.at[g, k])

    def cg(g, c):
        bs = [g * UC + u for u in range(UC)]
        t = [tile_of(xt, lhs, b) for b in bs]
        y = [first(vt, b, *x) for b, x in zip(bs, t)]
        z = [second(dw, b, *x, *w) for b, x, w in zip(bs, t, y)]
        for u, w in enumerate(z):
            spot = (g * (UC // 8) + u // 8, u % 8)
            total[spot] = iw[spot] + w
        for k in range(8):
            save(g, k).start()
        return c

    lax.fori_loop(0, NB // UC, cg, 0)
    for g in range(NB // UC):
        for k in range(8):
            save(g, k).wait()


def sublanes_last(x):
    return x.reshape(8, 8, -1, 128).transpose(0, 2, 1, 3)


def per_device(records, tool_data, owners, local_seg, active, stiffness, columns, vectors):
    vm, sm, dma = pltpu.VMEM, pltpu.SMEM, pltpu.SemaphoreType.DMA
    i32 = jnp.int32
    far = pl.BlockSpec(memory_space=pl.ANY)
    whole = pl.BlockSpec(memory_space=vm)
    parts = pl.pallas_call(
        gather_kernel,
        out_shape=(jax.ShapeDtypeStruct((NB, 8, 128), F32), jax.ShapeDtypeStruct((NB, 192, 64), BF16),
                   jax.ShapeDtypeStruct((NB, 64, 192), BF16), jax.ShapeDtypeStruct((NB, 32, 128), F32),
                   jax.ShapeDtypeStruct((8, 8, 32, 128), F32)),
        in_specs=[far] * 8,
        out_specs=(whole,) * 5,
        scratch_shapes=[
            vm((2, NB), i32), vm((2, NB), i32), vm((256, 512), F32), vm((8, 8, 32, 128), F32), sm((E5, NB), i32),
            vm((8, 8, 4, 128), F32), vm((NB, 64), i32), vm((E5, 8, 8, 32, 128), F32), vm((1, N), i32), sm((1, N), i32),
            vm((8, 16, 1, N), i32), vm((8, 16, 1, N), i32), vm((16, 8, 1, N), i32), vm((N, 8, 128), F32), vm((N, 8, 128), F32),
            vm((HB, 32, 128), F32), vm((HB, 32, 128), F32),
            vm((4, 64, 128), F32), vm((68, 128, 256), BF16), vm((64, 64), F32), vm((3, 4, 128, 64), F32), vm((256, 1536), BF16),
            dma((8,)), dma, dma, dma, dma, dma, dma, dma, dma, dma((16,)), dma((2 * HB,)), dma((2 * HB,)),
        ],
        compiler_params=pltpu.CompilerParams(collective_id=0, has_side_effects=True, vmem_limit_bytes=28 << 20),
        name="gather_rows",
    )(*[pltpu.with_memory_space_constraint(x, pltpu.HBM) for x in (owners.T, local_seg.T, tool_data, sublanes_last(vectors), columns.T, sublanes_last(records), active,
      stiffness.transpose(1, 0, 2).reshape(E5, 8, 8, 32, 128).transpose(0, 1, 3, 2, 4))])
    out = pl.pallas_call(
        contact_kernel,
        out_shape=jax.ShapeDtypeStruct((8, 32, 8, 128), F32),
        in_specs=[whole] * 5,
        out_specs=far,
        scratch_shapes=[vm((8, 8, 32, 128), F32), dma((NB // UC, 8))],
        compiler_params=pltpu.CompilerParams(vmem_limit_bytes=24 << 20),
        name="contact",
    )(*parts)
    return out.transpose(0, 2, 1, 3).reshape(NB, 4096)


def solution(mesh):
    ax = P(("dom", "tool"), None)
    return jax.shard_map(per_device, mesh=mesh, in_specs=(ax,) * 5 + (P(("dom", "tool"), None, None), ax, ax), out_specs=ax, check_vma=False)
```

```python
import math
import jax
import jax.numpy as jnp
import numpy as np
from jax import lax
from jax.experimental import pallas as pl
from jax.experimental.pallas import tpu as pltpu
from jax.sharding import PartitionSpec as P
F32, BF16 = jnp.float32, jnp.bfloat16
NB, HB, E5 = 64, 2, 5
A2 = math.log2(math.e) / 8.0
TURN = 1.0 / (2.0 * math.pi)
def fit():
    r = np.cos(np.linspace(0, np.pi / 2, 4001))[:-1] * 0.5
    w = np.sqrt(2.0) * np.sin(np.pi * r) / r
    a = np.stack([r ** (2 * k) for k in range(5)], 1)
    c = np.linalg.lstsq(a * r[:, None], w * r, rcond=None)[0]
    return [float(x) for x in c]


SINC = fit()

def iota(shape, dim):
    return lax.broadcasted_iota(jnp.int32, shape, dim)

def split(x):
    hi = x.astype(BF16)
    return hi, (x - hi.astype(F32)).astype(BF16)

def split3(x):
    h = x.astype(BF16).astype(F32)
    y = x - h
    m = y.astype(BF16).astype(F32)
    return h, m, y - m

def pair8(g0, g1):
    lane = iota((4, 128), 1)
    ev = jnp.where(lane < 64, g0, pltpu.roll(g1, 64, 1))
    od = jnp.where(lane < 64, pltpu.roll(g0, 64, 1), g1)
    return jnp.concatenate([ev, od], 0)

def mask_rows(which):
    s = iota((8, 128), 0)
    m = s == which[0]
    for w in which[1:]:
        m = m | (s == w)
    return m

def square_sum(x):
    return jnp.sum(jnp.where(mask_rows((0, 1, 4)), x * x, 0.0), 0, keepdims=True) * A2

def prep_vec(w, nat, bv, c, own_b, vt, dw):
    lane = iota((32, 128), 1)
    wr = pltpu.roll(w, 64, 1)
    nat[pl.ds(0, 32, stride=2), :] = jnp.where(lane < 64, w, wr)
    nat[pl.ds(1, 32, stride=2), :] = jnp.where(lane < 64, wr, w)
    d = nat[...]
    lane2 = iota((64, 128), 1)
    h, l = split(d)
    z = jnp.zeros_like(h)
    lo, up = lane2 < 64, lane2 >= 64
    bv[c] = jnp.concatenate([jnp.concatenate([jnp.where(lo, h, z), jnp.where(lo, l, z)], 1),
                             jnp.concatenate([jnp.where(up, h, z), jnp.where(up, l, z)], 1)], 0)
    if own_b is not None:
        w = w * dw[own_b]
        t = jnp.concatenate([w[:, :64], w[:, 64:]], 0).T
        h, l = split(t)
        vt[own_b] = jnp.concatenate([jnp.concatenate([h, h], 1), jnp.concatenate([l, l], 1)], 0)

def prep_act(act, at, dw):
    at[...] = act[...].astype(F32).T
    a = jnp.concatenate([at[pl.ds(0, 32, stride=2), :], at[pl.ds(1, 32, stride=2), :]], 1).astype(BF16)
    row, col = iota((128, 128), 0), iota((128, 128), 1)
    same = (row // 64) == (col // 64)
    def one(g, carry):
        for k in range(16):
            b = g * 16 + k
            hot = jnp.where(same & (lax.rem(row, 64) == b), 1.0, 0.0).astype(BF16)
            dw[b] = jnp.dot(a, hot, preferred_element_type=F32)
        return carry
    lax.fori_loop(0, 4, one, 0)

def prep_part(rw, ft, lhs, g, k):
    p = pair8(rw[g // 4, lax.rem(g, 4) * 2], rw[g // 4, lax.rem(g, 4) * 2 + 1])
    sub = iota((8, 128), 0)
    pos = mask_rows((0, 1, 4))
    ph, pm, pl_ = split3(-square_sum(p))
    extra = jnp.where(sub < 3, -1.0, jnp.where(sub == 3, ph, jnp.where(sub == 4, pm, jnp.where(sub == 5, pl_, 0.0))))
    scale = jnp.where(pos, 2.0 * A2, jnp.where(sub == 7, 1.0, jnp.where(sub == 3, TURN, 3.0 * TURN)))
    h, m, l = split3(p * scale)
    zero = jnp.zeros_like(h)
    for n, mk in enumerate((pos, mask_rows((2, 3, 5, 6)), sub == 7)):
        hh, mm, ll = (jnp.where(mk, x, 0.0) for x in (h, m, l))
        f = jnp.concatenate([hh, hh, hh, mm, mm, ll, extra if n == 0 else zero, zero], 0)
        ft[n, k] = f.T
    for q in range(2):
        parts = []
        for n in range(3):
            for par in range(2):
                parts.append(ft[n, k, pl.ds(q * 64 + par, 32, stride=2), :])
        lhs[g * 2 + q] = jnp.concatenate(parts, 0).astype(BF16)

def inner_block(cols, sw, bv, b, bb):
    w = jnp.concatenate([sw[e, b // 8, bb] for e in range(E5)], 1)
    h, l = split(w)
    r = jnp.concatenate([bv[cols[e, b]] for e in range(E5)], 0)
    o = jnp.dot(jnp.concatenate([h, l], 0), r, preferred_element_type=F32)
    return (o[:32, :128] + o[:32, 128:]) + (o[32:, :128] + o[32:, 128:])


def cand_rows(got, s):
    x = got[s // 2]
    return jnp.where(lax.rem(s, 2) == 1, x[4:8], x[0:4])

def tile_of(xt, lhs, b):
    x = xt[b]
    sub = iota((8, 128), 0)
    h, m, l = split3(x)
    qh, qm, ql = split3(square_sum(x))
    extra = jnp.where(sub == 0, qh, jnp.where(sub == 1, qm, jnp.where(sub == 2, ql, jnp.where(sub < 6, 1.0, 0.0))))
    rhs = jnp.concatenate([h, m, l, h, m, h, extra, jnp.zeros_like(h)], 0).astype(BF16)
    z = jnp.dot(lhs[b], rhs, preferred_element_type=F32)
    x = z[64:128]
    r = x - jnp.round(x)
    r2 = r * r
    s = SINC[4]
    for c in SINC[3::-1]:
        s = s * r2 + c
    s = s * r
    tile = jnp.exp2(z[:64]) * (1.0 - s * s) * (jnp.tanh(z[128:]) * 0.5 + 1.0)
    return split(tile)

def first(vt, b, th, tl):
    y = jnp.dot(vt[b], jnp.concatenate([th, tl], 0), preferred_element_type=F32)
    return split(y[:64] + y[64:])

def second(dw, b, th, tl, ih, il):
    lhs = jnp.concatenate([jnp.concatenate([th, th], 1), jnp.concatenate([tl, tl], 1)], 0)
    o = lax.dot_general(lhs, jnp.concatenate([ih, il], 1), (((1,), (1,)), ((), ())), preferred_element_type=F32)
    o = o[:64] + o[64:]
    return jnp.concatenate([o[:32], o[32:]], 1) * (dw[b] * 0.05)

MESH = pl.DeviceIdType.MESH
N = 128
UC = 32
PV = 12
RINGS = (((1, 0), (3, 0), (0, 1), (0, 3), (0, 0)), ((2, 0), (0, 2), (1, 1), (1, 3), (3, 1), (3, 3)), ((2, 1), (2, 3), (1, 2), (3, 2)), ((2, 2),))


def rows8(g):
    return pl.ds(pl.multiple_of(g * 8, 8), 8)


def local(src, dst, sem):
    return pltpu.make_async_copy(src, dst, sem)


def remote(src, dst, send, recv, where):
    return pltpu.make_async_remote_copy(src, dst, send, recv, device_id=where, device_id_type=MESH)


def gather_kernel(own_h, seg_h, tool_h, vec_h, cols_h, rec_h, act_h, s_h, xt, lhs, vt, dw, iw,
                  own_v, seg_v, tool, vw, cols, rw, act, sw, slot_v, slot,
                  req_s, req_m, req_r, resp, got, lo, hi, nat, bv, at, ft, tool3,
                  ls, vs, fs, gs, ss1, rs1, ss2, rs2, ss3, rs3, hs, hr):
    loads = [local(a, b, ls.at[i]) for i, (a, b) in enumerate(
        ((own_h, own_v), (seg_h, seg_v), (act_h, act), (tool_h, tool), (cols_h, cols)))]
    for c in loads[:2]:
        c.start()
    dom, tl = lax.axis_index("dom"), lax.axis_index("tool")
    me = dom * 8 + tl
    px, py = dom // 4, lax.rem(dom, 4)
    span = [(lax.rem(px + a, 4) * 4 + lax.rem(py + b, 4), tl)
            for a, b in ((2, 2), (2, 1), (2, 3), (1, 2), (3, 2), (1, 1), (1, 3), (3, 1), (3, 3), (2, 0), (0, 2), (1, 0), (3, 0), (0, 1), (0, 3))]
    part = [(dom, lax.rem(tl + j, 8)) for j in (4, 3, 5, 2, 6, 1, 7)]
    nxt, prv = lax.rem(me + 1, N), lax.rem(me + N - 1, N)
    after, before = (nxt // 8, lax.rem(nxt, 8)), (prv // 8, lax.rem(prv, 8))
    barrier = pltpu.get_barrier_semaphore()
    for where in span + part + [after, before]:
        pl.semaphore_signal(barrier, inc=1, device_id=where, device_id_type=MESH)
    for c in loads[2:]:
        c.start()
    for k in range(8):
        local(vec_h.at[:, :, k], vw.at[:, k], vs).start()
    for k in range(8):
        local(rec_h.at[:, :, k], rw.at[:, k], fs).start()
    for k in range(8):
        local(s_h.at[:, :, :, k], sw.at[:, :, k], gs).start()
    loads[0].wait()
    loads[1].wait()
    own = jnp.concatenate([own_v[0:1, :], own_v[1:2, :]], axis=1)
    seg = jnp.concatenate([seg_v[0:1, :], seg_v[1:2, :]], axis=1)
    row, col = iota((N, N), 0), iota((N, N), 1)
    hit = jnp.broadcast_to(lax.rem(own, 8) * 16 + own // 8, (N, N)) == row
    key = jnp.broadcast_to(col[0:1] * 256 + seg, (N, N))
    kmin = jnp.min(jnp.where(hit, key, 1 << 20), axis=1, keepdims=True)
    kmax = jnp.max(jnp.where(hit, key, 0), axis=1, keepdims=True)
    req_s[...] = (jnp.where(col == 0, kmin, kmax) & 255).reshape(8, 16, 1, N)
    loads[3].wait()
    for k in range(4):
        for n, x in enumerate(split3(tool[k * 64:(k + 1) * 64, :])):
            tool3[k * 64:(k + 1) * 64, n * 512:(n + 1) * 512] = x.astype(BF16)
    loads[2].wait()
    prep_act(act, at, dw)
    pl.semaphore_wait(barrier, 24)
    local(req_s.at[tl], req_m.at[tl], rs1).start()
    for where in part:
        remote(req_s.at[where[1]], req_m.at[tl], ss1, rs1, where).start()
    halo = [remote(vec_h.at[7, :, 6 + k], lo.at[k], hs.at[k], hr.at[k], after) for k in range(HB)]
    halo += [remote(vec_h.at[0, :, k], hi.at[k], hs.at[HB + k], hr.at[HB + k], before) for k in range(HB)]
    for c in halo:
        c.start()
    slot_v[...] = own * 2 + jnp.sum(jnp.where(hit & (key != kmin), 1, 0), axis=0, keepdims=True)

    local(vw, vw, vs).wait()

    def pv(g, c):
        for u in range(4):
            b = g * 4 + u
            prep_vec(vw[g // 2, lax.rem(g, 2) * 4 + u], nat.at[u], bv, b + HB, b, vt, dw)
        return c

    lax.fori_loop(0, PV, pv, 0)
    local(req_m, req_m, rs1).wait()
    local(req_m.at[:, dom], req_r.at[dom], rs3.at[dom]).start()
    for where in span:
        remote(req_m.at[:, where[0]], req_r.at[dom], ss3, rs3.at[dom], where).start()
    keep = local(slot_v, slot, ls.at[7])
    keep.start()
    lax.fori_loop(PV, 16, pv, 0)
    for ring in RINGS:
        rows = [lax.rem(px + a, 4) * 4 + lax.rem(py + b, 4) for a, b in ring]
        for d in rows:
            local(req_r.at[d], req_r.at[d], rs3.at[d]).wait()
        n = len(rows) * 8
        ask = jnp.concatenate([req_r[d].reshape(8, N) for d in rows], 0)
        hot = jnp.concatenate([(iota((n, 256), 1) == ask[:, r:r + 1]).astype(F32) for r in range(2)], 0).astype(BF16)
        g = jnp.dot(hot, tool3[...], preferred_element_type=F32)
        g = (g[:, :512] + g[:, 512:1024]) + g[:, 1024:]
        for i, d in enumerate(rows):
            for r in range(2):
                for f in range(4):
                    resp[rows8(d), r * 4 + f, :] = g[r * n + i * 8:r * n + i * 8 + 8, f * 128:(f + 1) * 128]
        far = [d for d, at in zip(rows, ring) if at != (0, 0)]
        near = len(far) < len(rows)
        if near:
            local(resp.at[me], got.at[me], rs2).start()

        def reply(j, c, far=far, near=near):
            t = lax.rem(tl + j, 8)
            for d in far:
                remote(resp.at[d * 8 + t], got.at[me], ss2, rs2, (d, t)).start()
            return c

        def beside(j, c):
            t = lax.rem(tl + j, 8)
            remote(resp.at[dom * 8 + t], got.at[me], ss2, rs2, (dom, t)).start()
            return c

        lax.fori_loop(0, 8, reply, 0)
        if near:
            lax.fori_loop(1, 8, beside, 0)
    local(rw, rw, fs).wait()

    def pp(g, c):
        for u in range(4):
            prep_part(rw, ft, lhs, g * 4 + u, u)
        return c

    lax.fori_loop(0, 8, pp, 0)
    for c in halo:
        c.wait()

    @pl.when(me == 0)
    def _():
        lo[...] = jnp.zeros_like(lo)

    @pl.when(me == N - 1)
    def _():
        hi[...] = jnp.zeros_like(hi)

    for k in range(HB):
        prep_vec(lo[k], nat.at[k], bv, k, None, vt, dw)
        prep_vec(hi[k], nat.at[HB + k], bv, HB + NB + k, None, vt, dw)
    loads[4].wait()
    local(sw, sw, gs).wait()

    def ig(g, c):
        z = [inner_block(cols, sw, bv, g * 8 + u, u) for u in range(8)]
        for u in range(8):
            iw[g, u] = z[u]
        return c

    lax.fori_loop(0, 8, ig, 0)
    keep.wait()
    local(req_s.at[pl.ds(0, 7)], req_s.at[pl.ds(0, 7)], ss1).wait()
    local(req_r.at[pl.ds(0, 15)], req_r.at[pl.ds(0, 15)], ss3).wait()
    local(got, got, rs2).wait()

    def pick(g, c):
        for u in range(32):
            b = g * 32 + u
            xt[b] = pair8(cand_rows(got, slot[0, b]), cand_rows(got, slot[0, NB + b]))
        return c

    lax.fori_loop(0, 2, pick, 0)
    local(resp.at[pl.ds(0, N - 1)], resp.at[pl.ds(0, N - 1)], ss2).wait()


def contact_kernel(xt, lhs, vt, dw, iw, out_h, total, os):
    def save(g, k):
        return local(total.at[pl.ds(g * (UC // 8), UC // 8), k], out_h.at[pl.ds(g * (UC // 8), UC // 8), :, k], os.at[g, k])

    def cg(g, c):
        bs = [g * UC + u for u in range(UC)]
        t = [tile_of(xt, lhs, b) for b in bs]
        y = [first(vt, b, *x) for b, x in zip(bs, t)]
        z = [second(dw, b, *x, *w) for b, x, w in zip(bs, t, y)]
        for u, w in enumerate(z):
            spot = (g * (UC // 8) + u // 8, u % 8)
            total[spot] = iw[spot] + w
        for k in range(8):
            save(g, k).start()
        return c

    lax.fori_loop(0, NB // UC, cg, 0)
    for g in range(NB // UC):
        for k in range(8):
            save(g, k).wait()


def sublanes_last(x):
    return x.reshape(8, 8, -1, 128).transpose(0, 2, 1, 3)


def per_device(records, tool_data, owners, local_seg, active, stiffness, columns, vectors):
    vm, sm, dma = pltpu.VMEM, pltpu.SMEM, pltpu.SemaphoreType.DMA
    i32 = jnp.int32
    far = pl.BlockSpec(memory_space=pl.ANY)
    whole = pl.BlockSpec(memory_space=vm)
    parts = pl.pallas_call(
        gather_kernel,
        out_shape=(jax.ShapeDtypeStruct((NB, 8, 128), F32), jax.ShapeDtypeStruct((NB, 192, 64), BF16),
                   jax.ShapeDtypeStruct((NB, 128, 128), BF16), jax.ShapeDtypeStruct((NB, 32, 128), F32),
                   jax.ShapeDtypeStruct((8, 8, 32, 128), F32)),
        in_specs=[far] * 8,
        out_specs=(whole,) * 5,
        scratch_shapes=[
            vm((2, NB), i32), vm((2, NB), i32), vm((256, 512), F32), vm((8, 8, 32, 128), F32), sm((E5, NB), i32),
            vm((8, 8, 4, 128), F32), vm((NB, 64), i32), vm((E5, 8, 8, 32, 128), F32), vm((1, N), i32), sm((1, N), i32),
            vm((8, 16, 1, N), i32), vm((8, 16, 1, N), i32), vm((16, 8, 1, N), i32), vm((N, 8, 128), F32), vm((N, 8, 128), F32),
            vm((HB, 32, 128), F32), vm((HB, 32, 128), F32),
            vm((4, 64, 128), F32), vm((68, 128, 256), BF16), vm((64, 64), F32), vm((3, 4, 128, 64), F32), vm((256, 1536), BF16),
            dma((8,)), dma, dma, dma, dma, dma, dma, dma, dma, dma((16,)), dma((2 * HB,)), dma((2 * HB,)),
        ],
        compiler_params=pltpu.CompilerParams(collective_id=0, has_side_effects=True, vmem_limit_bytes=28 << 20),
        name="gather_rows",
    )(*[pltpu.with_memory_space_constraint(x, pltpu.HBM) for x in (owners.T, local_seg.T, tool_data, sublanes_last(vectors), columns.T, sublanes_last(records), active,
      stiffness.transpose(1, 0, 2).reshape(E5, 8, 8, 32, 128).transpose(0, 1, 3, 2, 4))])
    out = pl.pallas_call(
        contact_kernel,
        out_shape=jax.ShapeDtypeStruct((8, 32, 8, 128), F32),
        in_specs=[whole] * 5,
        out_specs=far,
        scratch_shapes=[vm((8, 8, 32, 128), F32), dma((NB // UC, 8))],
        compiler_params=pltpu.CompilerParams(vmem_limit_bytes=24 << 20),
        name="contact",
    )(*parts)
    return out.transpose(0, 2, 1, 3).reshape(NB, 4096)


def solution(mesh):
    ax = P(("dom", "tool"), None)
    return jax.shard_map(per_device, mesh=mesh, in_specs=(ax,) * 5 + (P(("dom", "tool"), None, None), ax, ax), out_specs=ax, check_vma=False)
```

```python
import math
import jax
import jax.numpy as jnp
import numpy as np
from jax import lax
from jax.experimental import pallas as pl
from jax.experimental.pallas import tpu as pltpu
from jax.sharding import PartitionSpec as P
F32, BF16 = jnp.float32, jnp.bfloat16
NB, HB, E5 = 64, 2, 5
A2 = math.log2(math.e) / 8.0
TURN = 1.0 / (2.0 * math.pi)
def fit():
    r = np.cos(np.linspace(0, np.pi / 2, 4001))[:-1] * 0.5
    w = np.sqrt(2.0) * np.sin(np.pi * r) / r
    a = np.stack([r ** (2 * k) for k in range(5)], 1)
    c = np.linalg.lstsq(a * r[:, None], w * r, rcond=None)[0]
    return [float(x) for x in c]


SINC = fit()

def iota(shape, dim):
    return lax.broadcasted_iota(jnp.int32, shape, dim)

def split(x):
    hi = x.astype(BF16)
    return hi, (x - hi.astype(F32)).astype(BF16)

def split3(x):
    h = x.astype(BF16).astype(F32)
    y = x - h
    m = y.astype(BF16).astype(F32)
    return h, m, y - m

def pair8(g0, g1):
    lane = iota((4, 128), 1)
    ev = jnp.where(lane < 64, g0, pltpu.roll(g1, 64, 1))
    od = jnp.where(lane < 64, pltpu.roll(g0, 64, 1), g1)
    return jnp.concatenate([ev, od], 0)

def mask_rows(which):
    s = iota((8, 128), 0)
    m = s == which[0]
    for w in which[1:]:
        m = m | (s == w)
    return m

def square_sum(x):
    return jnp.sum(jnp.where(mask_rows((0, 1, 4)), x * x, 0.0), 0, keepdims=True) * A2

def prep_vec(w, nat, bv, c, own_b, vt, dw):
    lane = iota((32, 128), 1)
    wr = pltpu.roll(w, 64, 1)
    nat[pl.ds(0, 32, stride=2), :] = jnp.where(lane < 64, w, wr)
    nat[pl.ds(1, 32, stride=2), :] = jnp.where(lane < 64, wr, w)
    d = nat[...]
    lane2 = iota((64, 128), 1)
    h, l = split(d)
    z = jnp.zeros_like(h)
    lo, up = lane2 < 64, lane2 >= 64
    bv[c] = jnp.concatenate([jnp.concatenate([jnp.where(lo, h, z), jnp.where(lo, l, z)], 1),
                             jnp.concatenate([jnp.where(up, h, z), jnp.where(up, l, z)], 1)], 0)
    if own_b is not None:
        w = w * dw[own_b]
        t = jnp.concatenate([w[:, :64], w[:, 64:]], 0).T
        h, l = split(t)
        vt[own_b] = jnp.concatenate([jnp.concatenate([h, h], 1), jnp.concatenate([l, l], 1)], 0)

def prep_act(act, at, dw):
    at[...] = act[...].astype(F32).T
    a = jnp.concatenate([at[pl.ds(0, 32, stride=2), :], at[pl.ds(1, 32, stride=2), :]], 1).astype(BF16)
    row, col = iota((128, 128), 0), iota((128, 128), 1)
    same = (row // 64) == (col // 64)
    def one(g, carry):
        for k in range(16):
            b = g * 16 + k
            hot = jnp.where(same & (lax.rem(row, 64) == b), 1.0, 0.0).astype(BF16)
            dw[b] = jnp.dot(a, hot, preferred_element_type=F32)
        return carry
    lax.fori_loop(0, 4, one, 0)

def prep_part(rw, ft, lhs, g, k):
    p = pair8(rw[g // 4, lax.rem(g, 4) * 2], rw[g // 4, lax.rem(g, 4) * 2 + 1])
    sub = iota((8, 128), 0)
    pos = mask_rows((0, 1, 4))
    ph, pm, pl_ = split3(-square_sum(p))
    extra = jnp.where(sub < 3, -1.0, jnp.where(sub == 3, ph, jnp.where(sub == 4, pm, jnp.where(sub == 5, pl_, 0.0))))
    scale = jnp.where(pos, 2.0 * A2, jnp.where(sub == 7, 1.0, jnp.where(sub == 3, TURN, 3.0 * TURN)))
    h, m, l = split3(p * scale)
    zero = jnp.zeros_like(h)
    for n, mk in enumerate((pos, mask_rows((2, 3, 5, 6)), sub == 7)):
        hh, mm, ll = (jnp.where(mk, x, 0.0) for x in (h, m, l))
        f = jnp.concatenate([hh, hh, hh, mm, mm, ll, extra if n == 0 else zero, zero], 0)
        ft[n, k] = f.T
    for q in range(2):
        parts = []
        for n in range(3):
            for par in range(2):
                parts.append(ft[n, k, pl.ds(q * 64 + par, 32, stride=2), :])
        lhs[g * 2 + q] = jnp.concatenate(parts, 0).astype(BF16)

def inner_block(cols, sw, bv, b, bb):
    w = jnp.concatenate([sw[e, b // 8, bb] for e in range(E5)], 1)
    h, l = split(w)
    r = jnp.concatenate([bv[cols[e, b]] for e in range(E5)], 0)
    o = jnp.dot(jnp.concatenate([h, l], 0), r, preferred_element_type=F32)
    return (o[:32, :128] + o[:32, 128:]) + (o[32:, :128] + o[32:, 128:])


def cand_rows(got, s):
    x = got[s // 2]
    return jnp.where(lax.rem(s, 2) == 1, x[4:8], x[0:4])

def tile_of(xt, lhs, b):
    x = xt[b]
    sub = iota((8, 128), 0)
    h, m, l = split3(x)
    qh, qm, ql = split3(square_sum(x))
    extra = jnp.where(sub == 0, qh, jnp.where(sub == 1, qm, jnp.where(sub == 2, ql, jnp.where(sub < 6, 1.0, 0.0))))
    rhs = jnp.concatenate([h, m, l, h, m, h, extra, jnp.zeros_like(h)], 0).astype(BF16)
    z = jnp.dot(lhs[b], rhs, preferred_element_type=F32)
    x = z[64:128]
    r = x - jnp.round(x)
    r2 = r * r
    s = SINC[4]
    for c in SINC[3::-1]:
        s = s * r2 + c
    s = s * r
    tile = jnp.exp2(z[:64]) * (1.0 - s * s) * (jnp.tanh(z[128:]) * 0.5 + 1.0)
    return split(tile)

def first(vt, b, th, tl):
    y = jnp.dot(vt[b], jnp.concatenate([th, tl], 0), preferred_element_type=F32)
    return split(y[:64] + y[64:])

def second(dw, b, th, tl, ih, il):
    lhs = jnp.concatenate([jnp.concatenate([th, th], 1), jnp.concatenate([tl, tl], 1)], 0)
    o = lax.dot_general(lhs, jnp.concatenate([ih, il], 1), (((1,), (1,)), ((), ())), preferred_element_type=F32)
    o = o[:64] + o[64:]
    return jnp.concatenate([o[:32], o[32:]], 1) * (dw[b] * 0.05)

MESH = pl.DeviceIdType.MESH
N = 128
UC = 64
PV = 12
RINGS = (((1, 0), (3, 0), (0, 1), (0, 3), (0, 0)), ((2, 0), (0, 2), (1, 1), (1, 3), (3, 1), (3, 3)), ((2, 1), (2, 3), (1, 2), (3, 2)), ((2, 2),))


def rows8(g):
    return pl.ds(pl.multiple_of(g * 8, 8), 8)


def local(src, dst, sem):
    return pltpu.make_async_copy(src, dst, sem)


def remote(src, dst, send, recv, where):
    return pltpu.make_async_remote_copy(src, dst, send, recv, device_id=where, device_id_type=MESH)


def gather_kernel(own_h, seg_h, tool_h, vec_h, cols_h, rec_h, act_h, s_h, xt, lhs, vt, dw, iw,
                  own_v, seg_v, tool, vw, cols, rw, act, sw, slot_v, slot,
                  req_s, req_m, req_r, resp, got, lo, hi, nat, bv, at, ft, tool3,
                  ls, vs, fs, gs, ss1, rs1, ss2, rs2, ss3, rs3, hs, hr):
    loads = [local(a, b, ls.at[i]) for i, (a, b) in enumerate(
        ((own_h, own_v), (seg_h, seg_v), (act_h, act), (tool_h, tool), (cols_h, cols)))]
    for c in loads[:2]:
        c.start()
    dom, tl = lax.axis_index("dom"), lax.axis_index("tool")
    me = dom * 8 + tl
    px, py = dom // 4, lax.rem(dom, 4)
    span = [(lax.rem(px + a, 4) * 4 + lax.rem(py + b, 4), tl)
            for a, b in ((2, 2), (2, 1), (2, 3), (1, 2), (3, 2), (1, 1), (1, 3), (3, 1), (3, 3), (2, 0), (0, 2), (1, 0), (3, 0), (0, 1), (0, 3))]
    part = [(dom, lax.rem(tl + j, 8)) for j in (4, 3, 5, 2, 6, 1, 7)]
    nxt, prv = lax.rem(me + 1, N), lax.rem(me + N - 1, N)
    after, before = (nxt // 8, lax.rem(nxt, 8)), (prv // 8, lax.rem(prv, 8))
    barrier = pltpu.get_barrier_semaphore()
    for where in part + [after, before] + span:
        pl.semaphore_signal(barrier, inc=1, device_id=where, device_id_type=MESH)
    for c in loads[2:]:
        c.start()
    for k in range(8):
        local(vec_h.at[:, :, k], vw.at[:, k], vs).start()
    for k in range(8):
        local(rec_h.at[:, :, k], rw.at[:, k], fs).start()
    for k in range(8):
        local(s_h.at[:, :, :, k], sw.at[:, :, k], gs).start()
    loads[0].wait()
    loads[1].wait()
    own = jnp.concatenate([own_v[0:1, :], own_v[1:2, :]], axis=1)
    seg = jnp.concatenate([seg_v[0:1, :], seg_v[1:2, :]], axis=1)
    row, col = iota((N, N), 0), iota((N, N), 1)
    hit = jnp.broadcast_to(lax.rem(own, 8) * 16 + own // 8, (N, N)) == row
    key = jnp.broadcast_to(col[0:1] * 256 + seg, (N, N))
    kmin = jnp.min(jnp.where(hit, key, 1 << 20), axis=1, keepdims=True)
    kmax = jnp.max(jnp.where(hit, key, 0), axis=1, keepdims=True)
    req_s[...] = (jnp.where(col == 0, kmin, kmax) & 255).reshape(8, 16, 1, N)
    loads[3].wait()
    for k in range(4):
        for n, x in enumerate(split3(tool[k * 64:(k + 1) * 64, :])):
            tool3[k * 64:(k + 1) * 64, n * 512:(n + 1) * 512] = x.astype(BF16)
    loads[2].wait()
    prep_act(act, at, dw)
    pl.semaphore_wait(barrier, 24)
    local(req_s.at[tl], req_m.at[tl], rs1).start()
    for where in part:
        remote(req_s.at[where[1]], req_m.at[tl], ss1, rs1, where).start()
    halo = [remote(vec_h.at[7, :, 6 + k], lo.at[k], hs.at[k], hr.at[k], after) for k in range(HB)]
    halo += [remote(vec_h.at[0, :, k], hi.at[k], hs.at[HB + k], hr.at[HB + k], before) for k in range(HB)]
    for c in halo:
        c.start()
    slot_v[...] = own * 2 + jnp.sum(jnp.where(hit & (key != kmin), 1, 0), axis=0, keepdims=True)

    local(vw, vw, vs).wait()

    def pv(g, c):
        for u in range(4):
            b = g * 4 + u
            prep_vec(vw[g // 2, lax.rem(g, 2) * 4 + u], nat.at[u], bv, b + HB, b, vt, dw)
        return c

    lax.fori_loop(0, PV, pv, 0)
    local(req_m, req_m, rs1).wait()
    local(req_m.at[:, dom], req_r.at[dom], rs3.at[dom]).start()
    for where in span:
        remote(req_m.at[:, where[0]], req_r.at[dom], ss3, rs3.at[dom], where).start()
    keep = local(slot_v, slot, ls.at[7])
    keep.start()
    lax.fori_loop(PV, 16, pv, 0)
    for ring in RINGS:
        rows = [lax.rem(px + a, 4) * 4 + lax.rem(py + b, 4) for a, b in ring]
        for d in rows:
            local(req_r.at[d], req_r.at[d], rs3.at[d]).wait()
        n = len(rows) * 8
        ask = jnp.concatenate([req_r[d].reshape(8, N) for d in rows], 0)
        hot = jnp.concatenate([(iota((n, 256), 1) == ask[:, r:r + 1]).astype(F32) for r in range(2)], 0).astype(BF16)
        g = jnp.dot(hot, tool3[...], preferred_element_type=F32)
        g = (g[:, :512] + g[:, 512:1024]) + g[:, 1024:]
        for i, d in enumerate(rows):
            for r in range(2):
                for f in range(4):
                    resp[rows8(d), r * 4 + f, :] = g[r * n + i * 8:r * n + i * 8 + 8, f * 128:(f + 1) * 128]
        far = [d for d, at in zip(rows, ring) if at != (0, 0)]
        near = len(far) < len(rows)
        if near:
            local(resp.at[me], got.at[me], rs2).start()

        def reply(j, c, far=far, near=near):
            t = lax.rem(tl + j, 8)
            for d in far:
                remote(resp.at[d * 8 + t], got.at[me], ss2, rs2, (d, t)).start()
            return c

        def beside(j, c):
            t = lax.rem(tl + j, 8)
            remote(resp.at[dom * 8 + t], got.at[me], ss2, rs2, (dom, t)).start()
            return c

        lax.fori_loop(0, 8, reply, 0)
        if near:
            lax.fori_loop(1, 8, beside, 0)
    local(rw, rw, fs).wait()

    def pp(g, c):
        for u in range(4):
            prep_part(rw, ft, lhs, g * 4 + u, u)
        return c

    lax.fori_loop(0, 8, pp, 0)
    for c in halo:
        c.wait()

    @pl.when(me == 0)
    def _():
        lo[...] = jnp.zeros_like(lo)

    @pl.when(me == N - 1)
    def _():
        hi[...] = jnp.zeros_like(hi)

    for k in range(HB):
        prep_vec(lo[k], nat.at[k], bv, k, None, vt, dw)
        prep_vec(hi[k], nat.at[HB + k], bv, HB + NB + k, None, vt, dw)
    loads[4].wait()
    local(sw, sw, gs).wait()

    def ig(g, c):
        z = [inner_block(cols, sw, bv, g * 8 + u, u) for u in range(8)]
        for u in range(8):
            iw[g, u] = z[u]
        return c

    lax.fori_loop(0, 8, ig, 0)
    keep.wait()
    local(req_s.at[pl.ds(0, 7)], req_s.at[pl.ds(0, 7)], ss1).wait()
    local(req_r.at[pl.ds(0, 15)], req_r.at[pl.ds(0, 15)], ss3).wait()
    local(got, got, rs2).wait()

    def pick(g, c):
        for u in range(32):
            b = g * 32 + u
            xt[b] = pair8(cand_rows(got, slot[0, b]), cand_rows(got, slot[0, NB + b]))
        return c

    lax.fori_loop(0, 2, pick, 0)
    local(resp.at[pl.ds(0, N - 1)], resp.at[pl.ds(0, N - 1)], ss2).wait()


def contact_kernel(xt, lhs, vt, dw, iw, out_h, total, os):
    def save(g, k):
        return local(total.at[pl.ds(g * (UC // 8), UC // 8), k], out_h.at[pl.ds(g * (UC // 8), UC // 8), :, k], os.at[g, k])

    def cg(g, c):
        bs = [g * UC + u for u in range(UC)]
        t = [tile_of(xt, lhs, b) for b in bs]
        y = [first(vt, b, *x) for b, x in zip(bs, t)]
        z = [second(dw, b, *x, *w) for b, x, w in zip(bs, t, y)]
        for u, w in enumerate(z):
            spot = (g * (UC // 8) + u // 8, u % 8)
            total[spot] = iw[spot] + w
        for k in range(8):
            save(g, k).start()
        return c

    lax.fori_loop(0, NB // UC, cg, 0)
    for g in range(NB // UC):
        for k in range(8):
            save(g, k).wait()


def sublanes_last(x):
    return x.reshape(8, 8, -1, 128).transpose(0, 2, 1, 3)


def per_device(records, tool_data, owners, local_seg, active, stiffness, columns, vectors):
    vm, sm, dma = pltpu.VMEM, pltpu.SMEM, pltpu.SemaphoreType.DMA
    i32 = jnp.int32
    far = pl.BlockSpec(memory_space=pl.ANY)
    whole = pl.BlockSpec(memory_space=vm)
    parts = pl.pallas_call(
        gather_kernel,
        out_shape=(jax.ShapeDtypeStruct((NB, 8, 128), F32), jax.ShapeDtypeStruct((NB, 192, 64), BF16),
                   jax.ShapeDtypeStruct((NB, 128, 128), BF16), jax.ShapeDtypeStruct((NB, 32, 128), F32),
                   jax.ShapeDtypeStruct((8, 8, 32, 128), F32)),
        in_specs=[far] * 8,
        out_specs=(whole,) * 5,
        scratch_shapes=[
            vm((2, NB), i32), vm((2, NB), i32), vm((256, 512), F32), vm((8, 8, 32, 128), F32), sm((E5, NB), i32),
            vm((8, 8, 4, 128), F32), vm((NB, 64), i32), vm((E5, 8, 8, 32, 128), F32), vm((1, N), i32), sm((1, N), i32),
            vm((8, 16, 1, N), i32), vm((8, 16, 1, N), i32), vm((16, 8, 1, N), i32), vm((N, 8, 128), F32), vm((N, 8, 128), F32),
            vm((HB, 32, 128), F32), vm((HB, 32, 128), F32),
            vm((4, 64, 128), F32), vm((68, 128, 256), BF16), vm((64, 64), F32), vm((3, 4, 128, 64), F32), vm((256, 1536), BF16),
            dma((8,)), dma, dma, dma, dma, dma, dma, dma, dma, dma((16,)), dma((2 * HB,)), dma((2 * HB,)),
        ],
        compiler_params=pltpu.CompilerParams(collective_id=0, has_side_effects=True, vmem_limit_bytes=28 << 20),
        name="gather_rows",
    )(*[pltpu.with_memory_space_constraint(x, pltpu.HBM) for x in (owners.T, local_seg.T, tool_data, sublanes_last(vectors), columns.T, sublanes_last(records), active,
      stiffness.transpose(1, 0, 2).reshape(E5, 8, 8, 32, 128).transpose(0, 1, 3, 2, 4))])
    out = pl.pallas_call(
        contact_kernel,
        out_shape=jax.ShapeDtypeStruct((8, 32, 8, 128), F32),
        in_specs=[whole] * 5,
        out_specs=far,
        scratch_shapes=[vm((8, 8, 32, 128), F32), dma((NB // UC, 8))],
        compiler_params=pltpu.CompilerParams(vmem_limit_bytes=24 << 20),
        name="contact",
    )(*parts)
    return out.transpose(0, 2, 1, 3).reshape(NB, 4096)


def solution(mesh):
    ax = P(("dom", "tool"), None)
    return jax.shard_map(per_device, mesh=mesh, in_specs=(ax,) * 5 + (P(("dom", "tool"), None, None), ax, ax), out_specs=ax, check_vma=False)
```
